128 devices in a mesh: row: 8 (over x_hi, y), col: 16 (over x_lo, z, core).
Axes of the slice: x: 4 (x_hi: 2, x_lo: 2; x = x_hi * 2 + x_lo), y: 4, z: 4, core: 2. Of those that a mesh axis runs over, the one named last changes fastest.
Arguments:
- ainv_top: float32 [8192, 8192], P('row', 'col'), may hold values from -6 to 6
- block_owner: int32 [64], replicated, may hold values from 0 to 63, as said below
- upper_list: int32 [32, 32], P('col'), may hold values from 0 to 63, as said below
- upper_len: int32 [32], P('col'), may hold values from 24 to 32
- upper_panel: float32 [32, 4096, 128], P('col', 'row'), may hold values from -0.09375 to 0.09375
- upper_dinv: float32 [32, 128, 128], P('col'), may hold values from -6 to 6
- lower_len: int32 [32], P('col'), may hold values from 16 to 32, as said below
- lower_panel: float32 [32, 4096, 128], P('col', 'row'), may hold values from -0.09375 to 0.09375
- lower_parent: float32 [32, 128, 128], P('col'), may hold values from -0.5 to 0.5
- lower_dinv: float32 [32, 128, 128], P('col'), may hold values from -6 to 6
Outputs:
- upper_offdiag: float32 [32, 128, 8192], P('col', None, 'row')
- upper_diag: float32 [32, 128, 128], P('col')
- lower_offdiag: float32 [32, 128, 8192], P('col', None, 'row')
- lower_parent_block: float32 [32, 128, 128], P('col')
- lower_diag: float32 [32, 128, 128], P('col')
The draws below stay inside these ranges and needn't reach their ends.
Inputs may be any that keep to these rules, and one draw needn't show every extreme that they name: `block_owner`: a permutation of the storage blocks. `upper_list`: each row holds 32 different logical top block indices; their storage blocks are exactly 2 of each run of 4 storage blocks that starts at a multiple of 4. `lower_len`: never more than upper_len of the same supernode.
All inputs are finite; a program needn't handle non-finite values.
Results may differ from the reference program's by a relative error of at most 0.0003.
Values sent between devices are 32-bit elements; how exact they have to be, the bound alone decides.
No kernel may reach another device: no remote copies, remote signals or barrier semaphores. Data moves between devices by JAX's collectives and lax.ppermute only.
A program may use at most 192 MiB of HBM per device.

```python
import jax
import jax.numpy as jnp
from jax import lax

B = 128
TOP_COLS = 4
NT = 64
P_SIZE = 32
SUPER = 32


def lengths_pair(key):
    base = jax.random.fold_in(key, 11)
    first_key, second_key = jax.random.split(base)
    upper = jax.random.randint(first_key, (SUPER,), P_SIZE - P_SIZE // 4, P_SIZE + 1)
    upper = upper.at[0].set(P_SIZE).at[1].set(P_SIZE - P_SIZE // 4)
    scaled = jax.random.randint(second_key, (SUPER,), 0, 1 << 20)
    lower = P_SIZE // 2 + scaled * (upper - P_SIZE // 2 + 1) // (1 << 20)
    lower = lower.at[0].set(P_SIZE).at[1].set(P_SIZE // 2)
    return (upper.astype(jnp.int32), lower.astype(jnp.int32))


def storage_plan(key):
    owner = jax.random.permutation(jax.random.fold_in(key, 3), NT).astype(jnp.int32)
    groups = NT // TOP_COLS
    pick_keys = jax.random.split(jax.random.fold_in(key, 5), SUPER * groups)
    picks = jax.vmap(lambda one_key: jax.random.permutation(one_key, TOP_COLS))(pick_keys)[:, :TOP_COLS // 2]
    picks = picks.reshape(SUPER, groups, TOP_COLS // 2) + (jnp.arange(groups, dtype=jnp.int32) * TOP_COLS)[None, :, None]
    slots = picks.reshape(SUPER, P_SIZE).astype(jnp.int32)
    order_keys = jax.random.split(jax.random.fold_in(key, 9), SUPER)
    shuffles = jax.vmap(lambda one_key: jax.random.permutation(one_key, P_SIZE))(order_keys)
    slots = jnp.take_along_axis(slots, shuffles, axis=1)
    inverse = jnp.zeros((NT,), jnp.int32).at[owner].set(jnp.arange(NT, dtype=jnp.int32))
    return (owner, inverse[slots].astype(jnp.int32))


def draw_block_owner(key, part):
    return storage_plan(key)[0]


def draw_upper_list(key, part):
    return storage_plan(key)[1]


def draw_upper_len(key, part):
    return lengths_pair(key)[0]


def draw_lower_len(key, part):
    return lengths_pair(key)[1]


def level_of(key, shape, cuts, low, top_value):
    level = 1.0
    for axis_at, blocks in cuts:
        draws = jax.random.uniform(jax.random.fold_in(jax.random.fold_in(key, 6), axis_at), (blocks,), jnp.float32, low / len(cuts), top_value / len(cuts))
        level = level * jnp.repeat(jnp.exp(draws), shape[axis_at] // blocks).reshape((-1,) + (1,) * (len(shape) - 1 - axis_at))
    return level


def bell_draw(own_key, dims, width, limit, cuts=(), kind=jnp.bfloat16):
    gain = level_of(own_key, dims, cuts, -0.22, 0.18) if cuts else 1.0
    entries = jax.random.normal(own_key, dims, jnp.float32) * width * gain
    return jnp.minimum(jnp.maximum(entries, -limit), limit).astype(kind)


def setup_inputs(seed: int = 0) -> dict:
    arg_keys = jax.random.split(jax.random.key(seed), 11)
    return {
        "ainv_top": bell_draw(arg_keys[0], (NT * B, NT * B), 1.0, 6.0, ((0, 8), (1, 16)), jnp.float32),
        "block_owner": draw_block_owner(jax.random.fold_in(arg_keys[10], 71), 0),
        "upper_list": draw_upper_list(jax.random.fold_in(arg_keys[10], 71), 0),
        "upper_len": draw_upper_len(jax.random.fold_in(arg_keys[10], 71), 0),
        "upper_panel": bell_draw(arg_keys[4], (SUPER, P_SIZE * B, B), (P_SIZE * B) ** -0.5, 0.09375, ((0, 16), (1, 8)), jnp.float32),
        "upper_dinv": bell_draw(arg_keys[5], (SUPER, B, B), 1.0, 6.0, ((0, 16),), jnp.float32),
        "lower_len": draw_lower_len(jax.random.fold_in(arg_keys[10], 71), 0),
        "lower_panel": bell_draw(arg_keys[7], (SUPER, P_SIZE * B, B), (P_SIZE * B) ** -0.5, 0.09375, ((0, 16), (1, 8)), jnp.float32),
        "lower_parent": bell_draw(arg_keys[8], (SUPER, B, B), B ** -0.5, 0.5, ((0, 16),), jnp.float32),
        "lower_dinv": bell_draw(arg_keys[9], (SUPER, B, B), 1.0, 6.0, ((0, 16),), jnp.float32),
    }


highest = lax.Precision.HIGHEST


def matmul(left, right):
    return jnp.dot(left, right, precision=highest, preferred_element_type=jnp.float32)


def reference(ainv_top, block_owner, upper_list, upper_len, upper_panel, upper_dinv, lower_len, lower_panel, lower_parent, lower_dinv):
    block_w = upper_dinv.shape[-1]
    inside = jnp.arange(block_w, dtype=jnp.int32)
    places = jnp.arange(upper_list.shape[1], dtype=jnp.int32)
    total_cols = ainv_top.shape[1]

    def one_node(items):
        names, upper_count, upper_full, upper_inv, lower_count, lower_full, parent_block, lower_inv = items
        slots = block_owner[names].astype(jnp.int32)
        rows = (slots[:, None] * block_w + inside[None, :]).reshape(-1)
        chosen = jnp.take(jnp.take(ainv_top, rows, axis=0), rows, axis=1)
        keep_up = jnp.repeat((places < upper_count).astype(jnp.float32), block_w)[:, None]
        keep_low = jnp.repeat((places < lower_count).astype(jnp.float32), block_w)[:, None]
        panel_up = upper_full * keep_up
        panel_low = lower_full * keep_low
        g_up = -matmul(chosen, panel_up) * keep_up
        diag_up = upper_inv - matmul(panel_up.T, g_up)
        g_low = -(matmul(chosen, panel_low) + matmul(g_up, parent_block)) * keep_low
        parent_row = -(matmul(diag_up, parent_block) + matmul(g_up.T, panel_low))
        diag_low = lower_inv - matmul(parent_block.T, parent_row) - matmul(panel_low.T, g_low)
        off_up = jnp.zeros((block_w, total_cols), jnp.float32).at[:, rows].set(g_up.T)
        off_low = jnp.zeros((block_w, total_cols), jnp.float32).at[:, rows].set(g_low.T)
        return off_up, diag_up, off_low, parent_row, diag_low

    outputs = lax.map(one_node, (upper_list, upper_len, upper_panel, upper_dinv, lower_len, lower_panel, lower_parent, lower_dinv))
    return (outputs[0], outputs[1], outputs[2], outputs[3], outputs[4])
```

```python
import jax
import jax.numpy as jnp
from jax import lax
from jax.experimental import pallas as pl
from jax.experimental.pallas import tpu as pltpu
from jax.sharding import Mesh, PartitionSpec as P

B = 128
MIB = 1 << 20
ROW = ("xh", "y")
RING = ("xh", "xl")
f32 = jnp.float32
bf16 = jnp.bfloat16

smem = pl.BlockSpec(memory_space=pltpu.SMEM)
vmem = pl.BlockSpec(memory_space=pltpu.VMEM)
anyspace = pl.BlockSpec(memory_space=pl.ANY)


def params(mib):
    return pltpu.CompilerParams(vmem_limit_bytes=mib * MIB)


def shift(n, s):
    return [(i, (i + s) % n) for i in range(n)]


def swap_all(x, axis):
    return lax.all_to_all(x, axis, split_axis=0, concat_axis=0, tiled=True)


def split(x):
    hi = x.astype(bf16)
    return hi, (x - hi.astype(f32)).astype(bf16)


def dot(a, b):
    return jnp.dot(a, b, preferred_element_type=f32)


def dot3(a, b):
    ah, al = split(a)
    bh, bl = split(b)
    return dot(ah, bh) + (dot(ah, bl) + dot(al, bh))


def sort_slots(owner, names, node, inv, place, slot):
    def clear(t, _):
        inv[t] = -1
        return 0

    def mark(q, _):
        inv[owner[names[node, q]]] = q
        return 0

    def pick(g, _):
        t = 4 * g
        lo = jnp.where(inv[t] >= 0, 0, jnp.where(inv[t + 1] >= 0, 1, 2))
        hi = jnp.where(inv[t + 3] >= 0, 3, jnp.where(inv[t + 2] >= 0, 2, 1))
        place[2 * g] = inv[t + lo]
        slot[2 * g] = t + lo
        place[2 * g + 1] = inv[t + hi]
        slot[2 * g + 1] = t + hi
        return 0

    lax.fori_loop(0, 64, clear, 0)
    lax.fori_loop(0, 32, mark, 0)
    lax.fori_loop(0, 16, pick, 0)


def slice_kernel(up, low, out):
    for node in range(2):
        for q in range(4):
            for ul, src in enumerate((up, low)):
                for e in range(4):
                    out[node * 4 + q, (ul * 4 + e) * 32 : (ul * 4 + e + 1) * 32, :] = src[
                        node, e * B + q * 32 : e * B + (q + 1) * 32, :
                    ]


def order_kernel(pos, owner, names, ulen, llen, got, out, inv, place, slot):
    node = pos[0]
    sort_slots(owner, names, node, inv, place, slot)
    lens = (ulen[node], llen[node])
    lane = lax.broadcasted_iota(jnp.int32, (8, B), 1)
    info = jnp.zeros((8, B), f32)
    for s in range(32):
        h, q, e = s >> 4, (s >> 2) & 3, s & 3
        p = place[s]
        info = jnp.where(lane == s, slot[s].astype(f32), info)
        for ul in range(2):
            at = pl.multiple_of((ul * 4 + (p & 3)) * 32, 32)
            v = got[p >> 2, pl.ds(at, 32), :]
            v = jnp.where(p < lens[ul], v, 0.0)
            row = ((h * 4 + e) * 2 + ul) * 32
            out[q, row : row + 32, :] = v
    for q in range(4):
        out[q, 512:520, :] = info


def product_kernel(
    pos, slots, l0, lu, ld, lf1, lf2, a0, a1, a2, a3, a4, a5, a6, a7, a8, a9,
    o0, o1a, o1b, o2a, o2b, o3a, o3b,
    abuf, lhi, llo, selhi, sello, acc, sems, osems,
):
    x, y, z, core = pos[0] * 2 + pos[2], pos[1], pos[3], pos[4]
    whole = (a0, a1, a2, a3, None, None, a4, a5)
    copies = []
    for j, src in enumerate(whole):
        if src is not None:
            copies.append(pltpu.make_async_copy(src, abuf.at[j], sems.at[j]))
    for j, (top, bot) in ((4, (a6, a7)), (5, (a8, a9))):
        copies.append(pltpu.make_async_copy(top, abuf.at[j, :512], sems.at[j]))
        copies.append(pltpu.make_async_copy(bot, abuf.at[j, 512:], sems.at[j + 4]))
    for c in copies:
        c.start()

    def fill(node, src, row, ys):
        for e in range(8):
            for ul in range(2):
                hi, lo = split(src[row, (e * 2 + ul) * 32 : (e * 2 + ul + 1) * 32, :])
                at = pl.multiple_of(e * B + ys * 32, 32)
                lhi[node, pl.ds(at, 32), ul * B : (ul + 1) * B] = hi
                llo[node, pl.ds(at, 32), ul * B : (ul + 1) * B] = lo

    def fill_near(node, _):
        fill(node, l0, node, y)
        fill(node, lu, node, (y + 3) & 3)
        fill(node, ld, node, (y + 1) & 3)
        return 0

    def fill_far(i, _):
        fill(i, lf1, i, (y + 2) & 3)
        fill(i + 2, lf2, i, (y + 2) & 3)
        return 0

    lax.fori_loop(0, 4, fill_near, 0)
    lax.fori_loop(0, 2, fill_far, 0)
    for c in copies:
        c.wait()

    def step(t, _):
        j = t >> 2
        i = t & 3
        node = (z + i) & 3
        xs = (x + (j >> 1) * 3) & 3
        h = xs >> 1
        xl = xs & 1
        cs = (core + (j & 1)) & 1
        for b in range(2):
            ck = slots[node, 16 * xl + 4 * z + 2 * cs + b] & 3
            for m in range(4):
                cm = slots[node, 16 * h + 4 * y + m] & 7
                blk = abuf[j, pl.ds(pl.multiple_of(cm * B, B), B), pl.ds(pl.multiple_of(ck * B, B), B)]
                hi, lo = split(blk)
                selhi[m * B : (m + 1) * B, b * B : (b + 1) * B] = hi
                sello[m * B : (m + 1) * B, b * B : (b + 1) * B] = lo
        at = pl.multiple_of((xl * 4 + 2 * cs) * B, 2 * B)
        bh = lhi[node, pl.ds(at, 2 * B), :]
        bl = llo[node, pl.ds(at, 2 * B), :]
        r = dot(selhi[...], bh) + (dot(selhi[...], bl) + dot(sello[...], bh))

        first = (j == 0) | (j == 2 + 2 * (x & 1))

        @pl.when(first)
        def _():
            acc[i, h] = r

        @pl.when(jnp.logical_not(first))
        def _():
            acc[i, h] = acc[i, h] + r

        return 0

    lax.fori_loop(0, 32, step, 0)
    outs = ((o0.at[:512], 0, 0), (o0.at[512:], 0, 1), (o1a, 1, 0), (o1b, 1, 1),
            (o2a, 2, 0), (o2b, 2, 1), (o3a, 3, 0), (o3b, 3, 1))
    done = []
    for k, (dst, i, h) in enumerate(outs):
        done.append(pltpu.make_async_copy(acc.at[i, h], dst, osems.at[k]))
    for c in done:
        c.start()
    for c in done:
        c.wait()


def own_kernel(pos, o0, qa1, qa2, qb1, qb2, rows, mine, other, prods, lbuf):
    h, y = pos[0], pos[1]
    for e in range(8):
        for ul in range(2):
            for ys in range(4):
                lbuf[e * B + ys * 32 : e * B + (ys + 1) * 32, ul * B : (ul + 1) * B] = rows[
                    ys, (e * 2 + ul) * 32 : (e * 2 + ul + 1) * 32, :
                ]
    ya = -(o0[:512, :] + (qa1[...] + qa2[...]))
    yb = -(o0[512:, :] + (qb1[...] + qb2[...]))
    ta = ya.T
    tb = yb.T
    mine[...] = jnp.where(h == 0, ta, tb)
    other[...] = jnp.where(h == 0, tb, ta)
    la = lbuf[:512, :]
    lb = lbuf[512:, :]
    s = dot3(ta, la) + dot3(tb, lb)
    prods[0] = s[:B, :B]
    prods[1] = s[:B, B:]
    prods[2] = s[B:, B:]


def rows_kernel(pos, owner, names, ulen, llen, mine, other, parent, up, low, inv, place, slot):
    h, y = pos[0], pos[1]
    r = h * 4 + y
    up[...] = jnp.zeros_like(up)
    low[...] = jnp.zeros_like(low)
    for k, src in ((0, mine), (1, other)):
        node = h if k == 0 else 1 - h
        sort_slots(owner, names, node, inv, place, slot)
        lp = parent[node].T
        for e in range(4):
            p = place[4 * r + e]
            at = pl.multiple_of((slot[4 * r + e] & 7) * B, B)
            gu = jnp.where(p < ulen[node], src[:B, e * B : (e + 1) * B], 0.0)
            gl = src[B:, e * B : (e + 1) * B] - dot3(lp, gu)
            gl = jnp.where(p < llen[node], gl, 0.0)
            up[node, :, pl.ds(at, B)] = gu
            low[node, :, pl.ds(at, B)] = gl


def diag_kernel(pos, mine, other, uinv, linv, parent, du, pr, dl):
    h = pos[0]
    for k, src in ((0, mine), (1, other)):
        node = h if k == 0 else 1 - h
        lp = parent[node]
        lpt = lp.T
        cross = src[1]
        d = uinv[node] - src[0].T
        row = -(dot3(d, lp) + cross)
        low = src[2].T - dot3(cross.T, lp)
        du[node] = d
        pr[node] = row
        dl[node] = linv[node] - dot3(lpt, row) - low


def call(kernel, out_shape, in_specs, out_specs, scratch=(), mib=16, name=None):
    return pl.pallas_call(
        kernel,
        out_shape=out_shape,
        in_specs=in_specs,
        out_specs=out_specs,
        scratch_shapes=list(scratch),
        compiler_params=params(mib),
        name=name,
    )


def shape(*s):
    return jax.ShapeDtypeStruct(s, f32)


def body(
    ainv_top,
    block_owner,
    upper_list,
    upper_len,
    upper_panel,
    upper_dinv,
    lower_len,
    lower_panel,
    lower_parent,
    lower_dinv,
):
    pos = jnp.stack([lax.axis_index(n) for n in ("xh", "y", "xl", "z", "core")]).astype(jnp.int32)
    ints = pltpu.SMEM((64,), jnp.int32)
    pp = lax.ppermute
    sliced = call(slice_kernel, shape(8, 256, B), [vmem, vmem], vmem, name="slices")(upper_panel, lower_panel)
    got = swap_all(sliced, ROW)
    a = ainv_top
    a_up = pp(a, RING, shift(4, 1))
    a_dn = pp(a, RING, shift(4, 3))
    a_co = pp(a, "core", shift(2, 1))
    ordered = call(
        order_kernel, shape(4, 520, B), [smem] * 5 + [vmem], vmem, [ints, ints, ints], name="order"
    )(pos, block_owner, upper_list, upper_len, lower_len, got)
    l0 = swap_all(ordered, "z")
    lu = pp(l0, "y", shift(4, 1))
    ld = pp(l0, "y", shift(4, 3))
    lu, ld, a_up, a_dn = lax.optimization_barrier((lu, ld, a_up, a_dn))
    a_f1 = pp(a_up[:512], RING, shift(4, 1))
    a_f2 = pp(a_dn[512:], RING, shift(4, 3))
    lf1 = pp(lu[:2], "y", shift(4, 1))
    lf2 = pp(ld[2:], "y", shift(4, 3))
    c_up = pp(a_up, "core", shift(2, 1))
    c_dn = pp(a_dn, "core", shift(2, 1))
    c_f1 = pp(a_f1, "core", shift(2, 1))
    c_f2 = pp(a_f2, "core", shift(2, 1))
    ordered, lf1, lf2 = lax.optimization_barrier((ordered, lf1, lf2))
    rows = swap_all(ordered, "y")
    slots = l0[:, 512, :32].astype(jnp.int32)
    half = shape(512, 256)
    o0, o1a, o1b, o2a, o2b, o3a, o3b = call(
        product_kernel,
        [shape(1024, 256)] + [half] * 6,
        [smem] * 2 + [vmem] * 5 + [anyspace] * 10,
        [anyspace] * 7,
        [
            pltpu.VMEM((8, 1024, 512), f32),
            pltpu.VMEM((4, 1024, 256), bf16),
            pltpu.VMEM((4, 1024, 256), bf16),
            pltpu.VMEM((512, 256), bf16),
            pltpu.VMEM((512, 256), bf16),
            pltpu.VMEM((4, 2, 512, 256), f32),
            pltpu.SemaphoreType.DMA((10,)),
            pltpu.SemaphoreType.DMA((8,)),
        ],
        mib=48,
        name="product",
    )(pos, slots, l0, lu, ld, lf1, lf2, a, a_co, a_up, c_up, a_dn, c_dn, a_f1, a_f2, c_f1, c_f2)
    ra = pp(o2a, "z", shift(4, 1))
    rb = pp(o2b, "z", shift(4, 3))
    q1 = pp(o1b, "z", shift(4, 1))
    q2 = pp(o3a, "z", shift(4, 3))
    q3 = pp(o1a + ra, "z", shift(4, 1))
    q4 = pp(o3b + rb, "z", shift(4, 3))
    mine, other, prods = call(
        own_kernel,
        [shape(256, 512), shape(256, 512), shape(3, B, B)],
        [smem] + [vmem] * 6,
        [vmem] * 3,
        [pltpu.VMEM((1024, 256), f32)],
        mib=24,
        name="own",
    )(pos, o0, q3, q2, q1, q4, rows)
    s1 = pp(prods, "y", shift(4, 1))
    s2 = pp(prods, "y", shift(4, 2))
    s3 = pp(prods, "y", shift(4, 3))
    other = pp(other, "xh", shift(2, 1))
    mine_sum = (prods + s1) + (s2 + s3)
    other_sum = pp(mine_sum, "xh", shift(2, 1))
    upper_rows, lower_rows = call(
        rows_kernel,
        [shape(2, B, 1024)] * 2,
        [smem] * 5 + [vmem] * 3,
        [vmem] * 2,
        [ints, ints, ints],
        name="rows",
    )(pos, block_owner, upper_list, upper_len, lower_len, mine, other, lower_parent)
    diag_up, parent_row, diag_low = call(
        diag_kernel, [shape(2, B, B)] * 3, [smem] + [vmem] * 5, [vmem] * 3, name="diag"
    )(pos, mine_sum, other_sum, upper_dinv, lower_dinv, lower_parent)
    return (upper_rows, diag_up, lower_rows, parent_row, diag_low)


def solution(mesh):
    fine = Mesh(mesh.devices.reshape(2, 4, 2, 4, 2), ("xh", "y", "xl", "z", "core"))
    row = ("xh", "y")
    col = ("xl", "z", "core")
    in_specs = (
        P(row, col),
        P(),
        P(col, None),
        P(col),
        P(col, row, None),
        P(col, None, None),
        P(col),
        P(col, row, None),
        P(col, None, None),
        P(col, None, None),
    )
    out_specs = (
        P(col, None, row),
        P(col, None, None),
        P(col, None, row),
        P(col, None, None),
        P(col, None, None),
    )
    return jax.shard_map(body, mesh=fine, in_specs=in_specs, out_specs=out_specs, check_vma=False)
```

```python
import jax
import jax.numpy as jnp
from jax import lax
from jax.experimental import pallas as pl
from jax.experimental.pallas import tpu as pltpu
from jax.sharding import Mesh, PartitionSpec as P

B = 128
MIB = 1 << 20
ROW = ("xh", "y")
RING = ("xh", "xl")
f32 = jnp.float32
bf16 = jnp.bfloat16

smem = pl.BlockSpec(memory_space=pltpu.SMEM)
vmem = pl.BlockSpec(memory_space=pltpu.VMEM)
anyspace = pl.BlockSpec(memory_space=pl.ANY)


def params(mib):
    return pltpu.CompilerParams(vmem_limit_bytes=mib * MIB)


def shift(n, s):
    return [(i, (i + s) % n) for i in range(n)]


def swap_all(x, axis):
    return lax.all_to_all(x, axis, split_axis=0, concat_axis=0, tiled=True)


def split(x):
    hi = x.astype(bf16)
    return hi, (x - hi.astype(f32)).astype(bf16)


def dot(a, b):
    return jnp.dot(a, b, preferred_element_type=f32)


def dot3(a, b):
    ah, al = split(a)
    bh, bl = split(b)
    return dot(ah, bh) + (dot(ah, bl) + dot(al, bh))


def sort_slots(owner, names, node, inv, place, slot):
    def clear(t, _):
        inv[t] = -1
        return 0

    def mark(q, _):
        inv[owner[names[node, q]]] = q
        return 0

    def pick(g, _):
        t = 4 * g
        lo = jnp.where(inv[t] >= 0, 0, jnp.where(inv[t + 1] >= 0, 1, 2))
        hi = jnp.where(inv[t + 3] >= 0, 3, jnp.where(inv[t + 2] >= 0, 2, 1))
        place[2 * g] = inv[t + lo]
        slot[2 * g] = t + lo
        place[2 * g + 1] = inv[t + hi]
        slot[2 * g + 1] = t + hi
        return 0

    lax.fori_loop(0, 64, clear, 0)
    lax.fori_loop(0, 32, mark, 0)
    lax.fori_loop(0, 16, pick, 0)


def slice_kernel(up, low, out):
    for node in range(2):
        for q in range(4):
            for ul, src in enumerate((up, low)):
                for e in range(4):
                    out[node * 4 + q, (ul * 4 + e) * 32 : (ul * 4 + e + 1) * 32, :] = src[
                        node, e * B + q * 32 : e * B + (q + 1) * 32, :
                    ]


def order_kernel(pos, owner, names, ulen, llen, got, out, inv, place, slot):
    node = pos[0]
    sort_slots(owner, names, node, inv, place, slot)
    lens = (ulen[node], llen[node])
    lane = lax.broadcasted_iota(jnp.int32, (8, B), 1)
    info = jnp.zeros((8, B), f32)
    for s in range(32):
        h, q, e = s >> 4, (s >> 2) & 3, s & 3
        p = place[s]
        info = jnp.where(lane == s, slot[s].astype(f32), info)
        for ul in range(2):
            at = pl.multiple_of((ul * 4 + (p & 3)) * 32, 32)
            v = got[p >> 2, pl.ds(at, 32), :]
            v = jnp.where(p < lens[ul], v, 0.0)
            row = ((h * 4 + e) * 2 + ul) * 32
            out[q, row : row + 32, :] = v
    for q in range(4):
        out[q, 512:520, :] = info


def product_kernel(first, *refs):
    if first:
        (pos, slots, l0, lu, ld, lf1, lf2, own, own_c, up, up_c, dn, dn_c,
         o0, o1, o2, o3, hi_out, lo_out,
         abuf, lhi, llo, selhi, sello, acc, sems, osems, lsems) = refs
        outs = ((2, o2), (1, o1), (3, o3), (0, o0))
    else:
        (pos, slots, hi_in, lo_in, top, bot, top_c, bot_c, up, up_c, dn, dn_c,
         o0, o1a, o1b, o2a, o2b, o3a, o3b,
         abuf, lhi, llo, selhi, sello, acc, sems, osems, lsems) = refs
        outs = ((2, o2a, o2b), (1, o1a, o1b), (3, o3a, o3b), (0, o0))
    h, y, xl, z, core = pos[0], pos[1], pos[2], pos[3], pos[4]
    here = xl * 2 + core
    here_c = xl * 2 + 1 - core
    side = (1 - xl) * 2 + core
    side_c = (1 - xl) * 2 + 1 - core

    def fetch(src, dst, k):
        c = pltpu.make_async_copy(src, dst, sems.at[k])
        c.start()
        return c

    waits = []
    if first:
        waits.append(fetch(own, abuf.at[here], 0))
        waits.append(fetch(own_c, abuf.at[here_c], 1))
        from_dn = xl == 0
    else:
        loads = []
        for k, (src, dst) in enumerate(((hi_in, lhi), (lo_in, llo))):
            loads.append(pltpu.make_async_copy(src, dst, lsems.at[k]))
        waits.append(fetch(top, abuf.at[here, :512], 0))
        waits.append(fetch(bot, abuf.at[here, 512:], 4))
        waits.append(fetch(top_c, abuf.at[here_c, :512], 1))
        waits.append(fetch(bot_c, abuf.at[here_c, 512:], 5))
        from_dn = xl == 1

    @pl.when(from_dn)
    def _():
        fetch(dn, abuf.at[side], 2)
        fetch(dn_c, abuf.at[side_c], 3)

    @pl.when(jnp.logical_not(from_dn))
    def _():
        fetch(up, abuf.at[side], 2)
        fetch(up_c, abuf.at[side_c], 3)

    waits.append(pltpu.make_async_copy(up, abuf.at[side], sems.at[2]))
    waits.append(pltpu.make_async_copy(up_c, abuf.at[side_c], sems.at[3]))

    if first:

        def fill(node, src, row, ys):
            for e in range(8):
                for ul in range(2):
                    hi, lo = split(src[row, (e * 2 + ul) * 32 : (e * 2 + ul + 1) * 32, :])
                    at = pl.multiple_of(e * B + ys * 32, 32)
                    lhi[node, pl.ds(at, 32), ul * B : (ul + 1) * B] = hi
                    llo[node, pl.ds(at, 32), ul * B : (ul + 1) * B] = lo

        def fill_near(node, _):
            fill(node, l0, node, y)
            fill(node, lu, node, (y + 3) & 3)
            fill(node, ld, node, (y + 1) & 3)
            return 0

        def fill_far(i, _):
            fill(i, lf1, i, (y + 2) & 3)
            fill(i + 2, lf2, i, (y + 2) & 3)
            return 0

        lax.fori_loop(0, 4, fill_near, 0)
        lax.fori_loop(0, 2, fill_far, 0)
        loads = []
        for k, (src, dst) in enumerate(((lhi, hi_out), (llo, lo_out))):
            loads.append(pltpu.make_async_copy(src, dst, lsems.at[k]))
    for c in loads:
        c.start()
    for c in waits:
        c.wait()
    if not first:
        for c in loads:
            c.wait()

    m0 = 16 * (h if first else 1 - h) + 4 * y
    done = []
    for k, (i, *dst) in enumerate(outs):
        node = (z + i) & 3
        for m in range(4):
            cm = pl.multiple_of((slots[node, m0 + m] & 7) * B, B)
            for e in range(8):
                ck = slots[node, 16 * (e >> 2) + 4 * z + (e & 3)] & 3
                blk = abuf[e >> 1, pl.ds(cm, B), pl.ds(pl.multiple_of(ck * B, B), B)]
                hi, lo = split(blk)
                selhi[k & 1, m * B : (m + 1) * B, e * B : (e + 1) * B] = hi
                sello[k & 1, m * B : (m + 1) * B, e * B : (e + 1) * B] = lo
        bh = lhi[node]
        bl = llo[node]
        ah = selhi[k & 1]
        acc[i] = dot(ah, bh) + (dot(ah, bl) + dot(sello[k & 1], bh))
        rows = 512 // len(dst)
        for q, d in enumerate(dst):
            done.append(pltpu.make_async_copy(acc.at[i, q * rows : (q + 1) * rows], d, osems.at[len(done)]))
            done[-1].start()
    for c in done:
        c.wait()
    if first:
        for c in loads:
            c.wait()


def product(first, *args):
    n_l = 5 if first else 0
    half = [shape(512, 256)] * 4 if first else [shape(512, 256)] + [shape(256, 256)] * 6
    if first:
        half = half + [jax.ShapeDtypeStruct((4, 1024, 256), bf16)] * 2
    return call(
        lambda *refs: product_kernel(first, *refs),
        half,
        [smem] * 2 + [vmem] * n_l + [anyspace] * (len(args) - 2 - n_l),
        [anyspace] * len(half),
        [
            pltpu.VMEM((4, 1024, 512), f32),
            pltpu.VMEM((4, 1024, 256), bf16),
            pltpu.VMEM((4, 1024, 256), bf16),
            pltpu.VMEM((2, 512, 1024), bf16),
            pltpu.VMEM((2, 512, 1024), bf16),
            pltpu.VMEM((4, 512, 256), f32),
            pltpu.SemaphoreType.DMA((6,)),
            pltpu.SemaphoreType.DMA((8,)),
            pltpu.SemaphoreType.DMA((2,)),
        ],
        mib=40,
        name="product_own" if first else "product_far",
    )(*args)


def half_rows(h, rows):
    parts = []
    for e in range(4):
        for ys in range(4):
            both = []
            for ul in range(2):
                at = pl.multiple_of(((h * 4 + e) * 2 + ul) * 32, 32)
                both.append(rows[ys, pl.ds(at, 32), :])
            parts.append(jnp.concatenate(both, axis=1))
    return jnp.concatenate(parts, axis=0)


def near_kernel(pos, o0, q1, q2, q3, rows, mine, part):
    t = -((o0[...] + q1[...]) + (q2[...] + q3[...])).T
    mine[...] = t
    part[...] = dot3(t, half_rows(pos[0], rows))


def far_kernel(pos, o0, qa1, qa2, qb1, qb2, rows, part, other, prods):
    ya = o0[:256, :] + (qa1[...] + qa2[...])
    yb = o0[256:, :] + (qb1[...] + qb2[...])
    t = -jnp.concatenate([ya, yb], axis=0).T
    other[...] = t
    s = part[...] + dot3(t, half_rows(1 - pos[0], rows))
    prods[0] = s[:B, :B]
    prods[1] = s[:B, B:]
    prods[2] = s[B:, B:]


def rows_kernel(pos, owner, names, ulen, llen, mine, other, parent, up, low, inv, place, slot):
    h, y = pos[0], pos[1]
    r = h * 4 + y
    up[...] = jnp.zeros_like(up)
    low[...] = jnp.zeros_like(low)
    for k, src in ((0, mine), (1, other)):
        node = h if k == 0 else 1 - h
        sort_slots(owner, names, node, inv, place, slot)
        lp = parent[node].T
        for e in range(4):
            p = place[4 * r + e]
            at = pl.multiple_of((slot[4 * r + e] & 7) * B, B)
            gu = jnp.where(p < ulen[node], src[:B, e * B : (e + 1) * B], 0.0)
            gl = src[B:, e * B : (e + 1) * B] - dot3(lp, gu)
            gl = jnp.where(p < llen[node], gl, 0.0)
            up[node, :, pl.ds(at, B)] = gu
            low[node, :, pl.ds(at, B)] = gl


def diag_kernel(pos, mine, other, uinv, linv, parent, du, pr, dl):
    h = pos[0]
    for k, src in ((0, mine), (1, other)):
        node = h if k == 0 else 1 - h
        lp = parent[node]
        lpt = lp.T
        cross = src[1]
        d = uinv[node] - src[0].T
        row = -(dot3(d, lp) + cross)
        low = src[2].T - dot3(cross.T, lp)
        du[node] = d
        pr[node] = row
        dl[node] = linv[node] - dot3(lpt, row) - low


def call(kernel, out_shape, in_specs, out_specs, scratch=(), mib=16, name=None):
    return pl.pallas_call(
        kernel,
        out_shape=out_shape,
        in_specs=in_specs,
        out_specs=out_specs,
        scratch_shapes=list(scratch),
        compiler_params=params(mib),
        name=name,
    )


def shape(*s):
    return jax.ShapeDtypeStruct(s, f32)


def body(
    ainv_top,
    block_owner,
    upper_list,
    upper_len,
    upper_panel,
    upper_dinv,
    lower_len,
    lower_panel,
    lower_parent,
    lower_dinv,
):
    pos = jnp.stack([lax.axis_index(n) for n in ("xh", "y", "xl", "z", "core")]).astype(jnp.int32)
    ints = pltpu.SMEM((64,), jnp.int32)
    pp = lax.ppermute
    sliced = call(slice_kernel, shape(8, 256, B), [vmem, vmem], vmem, name="slices")(upper_panel, lower_panel)
    got = swap_all(sliced, ROW)
    a = ainv_top
    a_up = pp(a, RING, shift(4, 1))
    a_dn = pp(a, RING, shift(4, 3))
    a_co = pp(a, "core", shift(2, 1))
    ordered = call(
        order_kernel, shape(4, 520, B), [smem] * 5 + [vmem], vmem, [ints, ints, ints], name="order"
    )(pos, block_owner, upper_list, upper_len, lower_len, got)
    l0 = swap_all(ordered, "z")
    lu = pp(l0, "y", shift(4, 1))
    ld = pp(l0, "y", shift(4, 3))
    slots = l0[:, 512, :32].astype(jnp.int32)
    a_f1 = pp(a_up[:512], RING, shift(4, 1))
    a_f2 = pp(a_dn[512:], RING, shift(4, 3))
    lf1 = pp(lu[:2], "y", shift(4, 1))
    lf2 = pp(ld[2:], "y", shift(4, 3))
    k_up, k_dn, _, _ = lax.optimization_barrier((a_up, a_dn, lu, ld))
    c_up = pp(k_up, "core", shift(2, 1))
    c_dn = pp(k_dn, "core", shift(2, 1))
    c_f1 = pp(a_f1, "core", shift(2, 1))
    c_f2 = pp(a_f2, "core", shift(2, 1))
    n0, n1, n2, n3, hi, lo = product(
        True, pos, slots, l0, lu, ld, lf1, lf2, a, a_co, a_up, c_up, a_dn, c_dn
    )
    p1 = pp(n1, "z", shift(4, 1))
    p3 = pp(n3, "z", shift(4, 3))
    p2 = pp(n2, "z", shift(4, 2))
    ordered, _ = lax.optimization_barrier((ordered, n0))
    rows = swap_all(ordered, "y")
    a_f1, rows = lax.optimization_barrier((a_f1, rows))
    o0, o1a, o1b, o2a, o2b, o3a, o3b = product(
        False, pos, slots, hi, lo, a_f1, a_f2, c_f1, c_f2, a_up, c_up, a_dn, c_dn
    )
    ra = pp(o2a, "z", shift(4, 1))
    rb = pp(o2b, "z", shift(4, 3))
    q1 = pp(o1b, "z", shift(4, 1))
    q2 = pp(o3a, "z", shift(4, 3))
    q3 = pp(o1a + ra, "z", shift(4, 1))
    q4 = pp(o3b + rb, "z", shift(4, 3))
    mine, part = call(
        near_kernel, [shape(256, 512), shape(256, 256)], [smem] + [vmem] * 5, [vmem] * 2, mib=24, name="near"
    )(pos, n0, p1, p2, p3, rows)
    other, prods = call(
        far_kernel, [shape(256, 512), shape(3, B, B)], [smem] + [vmem] * 7, [vmem] * 2, mib=24, name="far"
    )(pos, o0, q3, q2, q1, q4, rows, part)
    s1 = pp(prods, "y", shift(4, 1))
    s2 = pp(prods, "y", shift(4, 2))
    s3 = pp(prods, "y", shift(4, 3))
    other = pp(other, "xh", shift(2, 1))
    mine_sum = (prods + s1) + (s2 + s3)
    other_sum = pp(mine_sum, "xh", shift(2, 1))
    upper_rows, lower_rows = call(
        rows_kernel,
        [shape(2, B, 1024)] * 2,
        [smem] * 5 + [vmem] * 3,
        [vmem] * 2,
        [ints, ints, ints],
        name="rows",
    )(pos, block_owner, upper_list, upper_len, lower_len, mine, other, lower_parent)
    other_sum, upper_rows = lax.optimization_barrier((other_sum, upper_rows))
    diag_up, parent_row, diag_low = call(
        diag_kernel, [shape(2, B, B)] * 3, [smem] + [vmem] * 5, [vmem] * 3, name="diag"
    )(pos, mine_sum, other_sum, upper_dinv, lower_dinv, lower_parent)
    return (upper_rows, diag_up, lower_rows, parent_row, diag_low)


def solution(mesh):
    fine = Mesh(mesh.devices.reshape(2, 4, 2, 4, 2), ("xh", "y", "xl", "z", "core"))
    row = ("xh", "y")
    col = ("xl", "z", "core")
    in_specs = (
        P(row, col),
        P(),
        P(col, None),
        P(col),
        P(col, row, None),
        P(col, None, None),
        P(col),
        P(col, row, None),
        P(col, None, None),
        P(col, None, None),
    )
    out_specs = (
        P(col, None, row),
        P(col, None, None),
        P(col, None, row),
        P(col, None, None),
        P(col, None, None),
    )
    return jax.shard_map(body, mesh=fine, in_specs=in_specs, out_specs=out_specs, check_vma=False)
```

```python
import jax
import jax.numpy as jnp
from jax import lax
from jax.experimental import pallas as pl
from jax.experimental.pallas import tpu as pltpu
from jax.sharding import Mesh, PartitionSpec as P

B = 128
MIB = 1 << 20
ROW = ("xh", "y")
RING = ("xh", "xl")
f32 = jnp.float32
bf16 = jnp.bfloat16

smem = pl.BlockSpec(memory_space=pltpu.SMEM)
vmem = pl.BlockSpec(memory_space=pltpu.VMEM)
anyspace = pl.BlockSpec(memory_space=pl.ANY)


def params(mib):
    return pltpu.CompilerParams(vmem_limit_bytes=mib * MIB)


def shift(n, s):
    return [(i, (i + s) % n) for i in range(n)]


def swap_all(x, axis):
    return lax.all_to_all(x, axis, split_axis=0, concat_axis=0, tiled=True)


def split(x):
    hi = x.astype(bf16)
    return hi, (x - hi.astype(f32)).astype(bf16)


def dot(a, b):
    return jnp.dot(a, b, preferred_element_type=f32)


def dot3(a, b):
    ah, al = split(a)
    bh, bl = split(b)
    return dot(ah, bh) + (dot(ah, bl) + dot(al, bh))


def sort_slots(owner, names, node, inv, place, slot):
    def clear(t, _):
        inv[t] = -1
        return 0

    def mark(q, _):
        inv[owner[names[node, q]]] = q
        return 0

    def pick(g, _):
        t = 4 * g
        lo = jnp.where(inv[t] >= 0, 0, jnp.where(inv[t + 1] >= 0, 1, 2))
        hi = jnp.where(inv[t + 3] >= 0, 3, jnp.where(inv[t + 2] >= 0, 2, 1))
        place[2 * g] = inv[t + lo]
        slot[2 * g] = t + lo
        place[2 * g + 1] = inv[t + hi]
        slot[2 * g + 1] = t + hi
        return 0

    lax.fori_loop(0, 64, clear, 0)
    lax.fori_loop(0, 32, mark, 0)
    lax.fori_loop(0, 16, pick, 0)


def slice_kernel(up, low, out):
    for node in range(2):
        for q in range(4):
            for ul, src in enumerate((up, low)):
                for e in range(4):
                    out[node * 4 + q, (ul * 4 + e) * 32 : (ul * 4 + e + 1) * 32, :] = src[
                        node, e * B + q * 32 : e * B + (q + 1) * 32, :
                    ]


def order_kernel(pos, owner, names, ulen, llen, got, out, v0, v1, v2, v3, inv, place, slot):
    node, y = pos[0], pos[1]
    sort_slots(owner, names, node, inv, place, slot)
    lens = (ulen[node], llen[node])
    lane = lax.broadcasted_iota(jnp.int32, (8, B), 1)
    info = jnp.zeros((8, B), f32)
    for s in range(32):
        h, q, e = s >> 4, (s >> 2) & 3, s & 3
        p = place[s]
        info = jnp.where(lane == s, slot[s].astype(f32), info)
        for ul in range(2):
            at = pl.multiple_of((ul * 4 + (p & 3)) * 32, 32)
            v = got[p >> 2, pl.ds(at, 32), :]
            v = jnp.where(p < lens[ul], v, 0.0)
            row = ((h * 4 + e) * 2 + ul) * 32
            out[q, row : row + 32, :] = v
    for q in range(4):
        out[q, 512:520, :] = info
    for i, v in enumerate((v0, v1, v2, v3)):
        v[...] = out[(y + i) & 3, :512, :]


def product_kernel(first, *refs):
    if first:
        (pos, slots, l0, lu, ld, lf1, lf2, own, own_c, side, side_c,
         o0, o1, o2, o3, lhi, llo, selhi, sello) = refs
        outs = ((2, o2), (1, o1), (3, o3), (0, o0))
        pieces = ((own,), (own_c,), (side,), (side_c,))
    else:
        (pos, slots, lhi, llo, top, bot, top_c, bot_c, side, side_c,
         o0, o1a, o1b, o2a, o2b, o3a, o3b, selhi, sello) = refs
        outs = ((2, o2a, o2b), (1, o1a, o1b), (3, o3a, o3b), (0, o0))
        pieces = ((top, bot), (top_c, bot_c), (side,), (side_c,))
    h, y, xl, z, core = pos[0], pos[1], pos[2], pos[3], pos[4]
    at_half = (xl, xl, 1 - xl, 1 - xl)
    at_pair = (core, 1 - core, core, 1 - core)

    if first:

        def fill(node, src, row, ys):
            for p in range(4):
                for b in range(2):
                    e = at_half[p] * 4 + at_pair[p] * 2 + b
                    for ul in range(2):
                        r = pl.multiple_of((e * 2 + ul) * 32, 32)
                        hi, lo = split(src[row, pl.ds(r, 32), :])
                        at = pl.multiple_of((p * 2 + b) * B + ys * 32, 32)
                        lhi[node, pl.ds(at, 32), ul * B : (ul + 1) * B] = hi
                        llo[node, pl.ds(at, 32), ul * B : (ul + 1) * B] = lo

        def fill_near(node, _):
            fill(node, l0, node, y)
            fill(node, lu, node, (y + 3) & 3)
            fill(node, ld, node, (y + 1) & 3)
            return 0

        def fill_far(i, _):
            fill(i, lf1, i, (y + 2) & 3)
            fill(i + 2, lf2, i, (y + 2) & 3)
            return 0

        lax.fori_loop(0, 4, fill_near, 0)
        lax.fori_loop(0, 2, fill_far, 0)

    m0 = 16 * (h if first else 1 - h) + 4 * y
    for k, (i, *dst) in enumerate(outs):
        node = (z + i) & 3
        for m in range(4):
            cm = slots[node, m0 + m] & 7
            for p in range(4):
                for b in range(2):
                    ck = slots[node, 16 * at_half[p] + 4 * z + 2 * at_pair[p] + b] & 3
                    lanes = pl.ds(pl.multiple_of(ck * B, B), B)
                    if len(pieces[p]) == 1:
                        blk = pieces[p][0][pl.ds(pl.multiple_of(cm * B, B), B), lanes]
                    else:
                        sub = pl.ds(pl.multiple_of((cm & 3) * B, B), B)
                        blk = jnp.where(cm < 4, pieces[p][0][sub, lanes], pieces[p][1][sub, lanes])
                    hi, lo = split(blk)
                    e = p * 2 + b
                    selhi[k & 1, m * B : (m + 1) * B, e * B : (e + 1) * B] = hi
                    sello[k & 1, m * B : (m + 1) * B, e * B : (e + 1) * B] = lo
        bh = lhi[node]
        bl = llo[node]
        ah = selhi[k & 1]
        r = dot(ah, bh) + (dot(ah, bl) + dot(sello[k & 1], bh))
        rows = 512 // len(dst)
        for q, d in enumerate(dst):
            d[...] = r[q * rows : (q + 1) * rows]


def product(first, *args):
    out = [shape(512, 256)] * 4 if first else [shape(512, 256)] + [shape(256, 256)] * 6
    if first:
        out = out + [jax.ShapeDtypeStruct((4, 1024, 256), bf16)] * 2
    return call(
        lambda *refs: product_kernel(first, *refs),
        out,
        [smem] * 2 + [vmem] * (len(args) - 2),
        [vmem] * len(out),
        [pltpu.VMEM((2, 512, 1024), bf16), pltpu.VMEM((2, 512, 1024), bf16)],
        mib=26,
        name="product_own" if first else "product_far",
    )(*args)


def half_rows(h, y, rows, buf):
    for e in range(4):
        for i, src in enumerate(rows):
            to = pl.multiple_of(e * B + ((y - i) & 3) * 32, 32)
            for ul in range(2):
                at = pl.multiple_of(((h * 4 + e) * 2 + ul) * 32, 32)
                buf[pl.ds(to, 32), ul * B : (ul + 1) * B] = src[pl.ds(at, 32), :]
    return buf[...]


def near_kernel(pos, o0, q1, q2, q3, v0, v1, v2, v3, mine, part, buf):
    t = -((o0[...] + q1[...]) + (q2[...] + q3[...])).T
    mine[...] = t
    part[...] = dot3(t, half_rows(pos[0], pos[1], (v0, v1, v2, v3), buf))


def far_kernel(pos, o0, qa1, qa2, qb1, qb2, v0, v1, v2, v3, part, other, prods, buf):
    ya = o0[:256, :] + (qa1[...] + qa2[...])
    yb = o0[256:, :] + (qb1[...] + qb2[...])
    t = -jnp.concatenate([ya, yb], axis=0).T
    other[...] = t
    s = part[...] + dot3(t, half_rows(1 - pos[0], pos[1], (v0, v1, v2, v3), buf))
    prods[0] = s[:B, :B]
    prods[1] = s[:B, B:]
    prods[2] = s[B:, B:]


def rows_kernel(pos, owner, names, ulen, llen, mine, other, parent, up, low, inv, place, slot):
    h, y = pos[0], pos[1]
    r = h * 4 + y
    up[...] = jnp.zeros_like(up)
    low[...] = jnp.zeros_like(low)
    for k, src in ((0, mine), (1, other)):
        node = h if k == 0 else 1 - h
        sort_slots(owner, names, node, inv, place, slot)
        lp = parent[node].T
        for e in range(4):
            p = place[4 * r + e]
            at = pl.multiple_of((slot[4 * r + e] & 7) * B, B)
            gu = jnp.where(p < ulen[node], src[:B, e * B : (e + 1) * B], 0.0)
            gl = src[B:, e * B : (e + 1) * B] - dot3(lp, gu)
            gl = jnp.where(p < llen[node], gl, 0.0)
            up[node, :, pl.ds(at, B)] = gu
            low[node, :, pl.ds(at, B)] = gl


def diag_kernel(pos, mine, other, uinv, linv, parent, du, pr, dl):
    h = pos[0]
    for k, src in ((0, mine), (1, other)):
        node = h if k == 0 else 1 - h
        lp = parent[node]
        lpt = lp.T
        cross = src[1]
        d = uinv[node] - src[0].T
        row = -(dot3(d, lp) + cross)
        low = src[2].T - dot3(cross.T, lp)
        du[node] = d
        pr[node] = row
        dl[node] = linv[node] - dot3(lpt, row) - low


def call(kernel, out_shape, in_specs, out_specs, scratch=(), mib=16, name=None):
    return pl.pallas_call(
        kernel,
        out_shape=out_shape,
        in_specs=in_specs,
        out_specs=out_specs,
        scratch_shapes=list(scratch),
        compiler_params=params(mib),
        name=name,
    )


def shape(*s):
    return jax.ShapeDtypeStruct(s, f32)


def body(
    ainv_top,
    block_owner,
    upper_list,
    upper_len,
    upper_panel,
    upper_dinv,
    lower_len,
    lower_panel,
    lower_parent,
    lower_dinv,
):
    pos = jnp.stack([lax.axis_index(n) for n in ("xh", "y", "xl", "z", "core")]).astype(jnp.int32)
    ints = pltpu.SMEM((64,), jnp.int32)
    pp = lax.ppermute
    mirror = [(0, 3), (1, 2), (2, 1), (3, 0)]
    sliced = call(slice_kernel, shape(8, 256, B), [vmem, vmem], vmem, name="slices")(upper_panel, lower_panel)
    got = swap_all(sliced, ROW)
    a = ainv_top
    a_nr = pp(a, "xl", shift(2, 1))
    a_fr = pp(a, RING, mirror)
    a_co = pp(a, "core", shift(2, 1))
    got, a_co = lax.optimization_barrier((got, a_co))
    ordered, v0, v1, v2, v3 = call(
        order_kernel,
        [shape(4, 520, B)] + [shape(512, B)] * 4,
        [smem] * 5 + [vmem],
        [vmem] * 5,
        [ints, ints, ints],
        name="order",
    )(pos, block_owner, upper_list, upper_len, lower_len, got)
    l0 = swap_all(ordered, "z")
    v1, v2, v3 = (pp(v, "y", shift(4, i + 1)) for i, v in enumerate((v1, v2, v3)))
    l0, v1, v2, v3 = lax.optimization_barrier((l0, v1, v2, v3))
    rows = (v0, v1, v2, v3)
    lu = pp(l0, "y", shift(4, 1))
    ld = pp(l0, "y", shift(4, 3))
    slots = l0[:, 512, :32].astype(jnp.int32)
    a_f1 = pp(a_nr[:512], RING, mirror)
    a_f2 = pp(a_fr[512:], "xl", shift(2, 1))
    a_nr, a_fr, lu, ld = lax.optimization_barrier((a_nr, a_fr, lu, ld))
    c_nr = pp(a_nr, "core", shift(2, 1))
    lf1 = pp(lu[:2], "y", shift(4, 1))
    lf2 = pp(ld[2:], "y", shift(4, 3))
    k_fr, lf1, lf2 = lax.optimization_barrier((a_fr, lf1, lf2))
    c_fr = pp(k_fr, "core", shift(2, 1))
    n0, n1, n2, n3, hi, lo = product(True, pos, slots, l0, lu, ld, lf1, lf2, a, a_co, a_nr, c_nr)
    a_f1, a_f2, n0 = lax.optimization_barrier((a_f1, a_f2, n0))
    c_f1 = pp(a_f1, "core", shift(2, 1))
    c_f2 = pp(a_f2, "core", shift(2, 1))
    p1 = pp(n1, "z", shift(4, 1))
    p3 = pp(n3, "z", shift(4, 3))
    p2 = pp(n2, "z", shift(4, 2))
    o0, o1a, o1b, o2a, o2b, o3a, o3b = product(
        False, pos, slots, hi, lo, a_f1, a_f2, c_f1, c_f2, a_fr, c_fr
    )
    ra = pp(o2a, "z", shift(4, 1))
    rb = pp(o2b, "z", shift(4, 3))
    q1 = pp(o1b, "z", shift(4, 1))
    q2 = pp(o3a, "z", shift(4, 3))
    q3 = pp(o1a + ra, "z", shift(4, 1))
    q4 = pp(o3b + rb, "z", shift(4, 3))
    lbuf = [pltpu.VMEM((512, 256), f32)]
    mine, part = call(
        near_kernel, [shape(256, 512), shape(256, 256)], [smem] + [vmem] * 8, [vmem] * 2, lbuf, mib=24, name="near"
    )(pos, n0, p1, p2, p3, *rows)
    other, prods = call(
        far_kernel, [shape(256, 512), shape(3, B, B)], [smem] + [vmem] * 10, [vmem] * 2, lbuf, mib=24, name="far"
    )(pos, o0, q3, q2, q1, q4, *rows, part)
    s1 = pp(prods, "y", shift(4, 1))
    s2 = pp(prods, "y", shift(4, 2))
    s3 = pp(prods, "y", shift(4, 3))
    other = pp(other, "xh", shift(2, 1))
    mine_sum = (prods + s1) + (s2 + s3)
    other_sum = pp(mine_sum, "xh", shift(2, 1))
    upper_rows, lower_rows = call(
        rows_kernel,
        [shape(2, B, 1024)] * 2,
        [smem] * 5 + [vmem] * 3,
        [vmem] * 2,
        [ints, ints, ints],
        name="rows",
    )(pos, block_owner, upper_list, upper_len, lower_len, mine, other, lower_parent)
    other_sum, upper_rows = lax.optimization_barrier((other_sum, upper_rows))
    diag_up, parent_row, diag_low = call(
        diag_kernel, [shape(2, B, B)] * 3, [smem] + [vmem] * 5, [vmem] * 3, name="diag"
    )(pos, mine_sum, other_sum, upper_dinv, lower_dinv, lower_parent)
    return (upper_rows, diag_up, lower_rows, parent_row, diag_low)


def solution(mesh):
    fine = Mesh(mesh.devices.reshape(2, 4, 2, 4, 2), ("xh", "y", "xl", "z", "core"))
    row = ("xh", "y")
    col = ("xl", "z", "core")
    in_specs = (
        P(row, col),
        P(),
        P(col, None),
        P(col),
        P(col, row, None),
        P(col, None, None),
        P(col),
        P(col, row, None),
        P(col, None, None),
        P(col, None, None),
    )
    out_specs = (
        P(col, None, row),
        P(col, None, None),
        P(col, None, row),
        P(col, None, None),
        P(col, None, None),
    )
    return jax.shard_map(body, mesh=fine, in_specs=in_specs, out_specs=out_specs, check_vma=False)
```

```python
import jax
import jax.numpy as jnp
from jax import lax
from jax.experimental import pallas as pl
from jax.experimental.pallas import tpu as pltpu
from jax.sharding import Mesh, PartitionSpec as P

B = 128
MIB = 1 << 20
ROW = ("xh", "y")
RING = ("xh", "xl")
f32 = jnp.float32
bf16 = jnp.bfloat16

smem = pl.BlockSpec(memory_space=pltpu.SMEM)
vmem = pl.BlockSpec(memory_space=pltpu.VMEM)
hbm = pl.BlockSpec(memory_space=pltpu.HBM)


def params(mib):
    return pltpu.CompilerParams(vmem_limit_bytes=mib * MIB)


def shift(n, s):
    return [(i, (i + s) % n) for i in range(n)]


def swap_all(x, axis):
    return lax.all_to_all(x, axis, split_axis=0, concat_axis=0, tiled=True)


def split(x):
    hi = x.astype(bf16)
    return hi, (x - hi.astype(f32)).astype(bf16)


def dot(a, b):
    return jnp.dot(a, b, preferred_element_type=f32)


def dot3(a, b):
    ah, al = split(a)
    bh, bl = split(b)
    return dot(ah, bh) + (dot(ah, bl) + dot(al, bh))


def sort_kernel(owner, names, place, slot, inv):
    for node in range(2):

        def clear(t, _):
            inv[t] = -1
            return 0

        def mark(q, _):
            inv[owner[names[node, q]]] = q
            return 0

        def pick(g, _):
            t = 4 * g
            lo = jnp.where(inv[t] >= 0, 0, jnp.where(inv[t + 1] >= 0, 1, 2))
            hi = jnp.where(inv[t + 3] >= 0, 3, jnp.where(inv[t + 2] >= 0, 2, 1))
            place[node, 2 * g] = inv[t + lo]
            slot[node, 2 * g] = t + lo
            place[node, 2 * g + 1] = inv[t + hi]
            slot[node, 2 * g + 1] = t + hi
            return 0

        lax.fori_loop(0, 64, clear, 0)
        lax.fori_loop(0, 32, mark, 0)
        lax.fori_loop(0, 16, pick, 0)


def slice_kernel(up, low, out, sem):
    copies = []
    for node in range(2):
        for q in range(4):
            for ul, src in enumerate((up, low)):
                copies.append(
                    pltpu.make_async_copy(src.at[node, :, q * 32 : (q + 1) * 32, :], out.at[node * 4 + q, ul], sem)
                )
    for c in copies:
        c.start()
    for c in copies:
        c.wait()


def order_kernel(pos, place, slot, ulen, llen, got, out, v0, v1, v2, v3, buf, sems):
    node, y = pos[0], pos[1]
    lens = (ulen[node], llen[node])
    lane = lax.broadcasted_iota(jnp.int32, (8, B), 1)
    info = jnp.zeros((8, B), f32)
    for s in range(32):
        info = jnp.where(lane == s, slot[node, s].astype(f32), info)
    copies = []
    for q in range(4):
        for h in range(2):
            for e in range(4):
                p = place[node, 16 * h + 4 * q + e]
                for ul in range(2):
                    at = pl.multiple_of((ul * 4 + (p & 3)) * 32, 32)
                    v = got[p >> 2, pl.ds(at, 32), :]
                    v = jnp.where(p < lens[ul], v, 0.0)
                    row = ((h * 4 + e) * 2 + ul) * 32
                    buf[q, row : row + 32, :] = v
        buf[q, 512:520, :] = info
        copies.append(pltpu.make_async_copy(buf.at[q], out.at[q], sems.at[q]))
        copies[-1].start()
    for i, v in enumerate((v0, v1, v2, v3)):
        copies.append(pltpu.make_async_copy(buf.at[(y + i) & 3, :512], v, sems.at[4 + i]))
        copies[-1].start()
    for c in copies:
        c.wait()


def fill(pos, lhi, llo, node, src, row, ys):
    xl, core = pos[2], pos[4]
    for p in range(4):
        half = xl if p < 2 else 1 - xl
        pair = core if p % 2 == 0 else 1 - core
        for b in range(2):
            e = half * 4 + pair * 2 + b
            for ul in range(2):
                r = pl.multiple_of((e * 2 + ul) * 32, 32)
                hi, lo = split(src[row, pl.ds(r, 32), :])
                at = pl.multiple_of((p * 2 + b) * B + ys * 32, 32)
                lhi[node, pl.ds(at, 32), ul * B : (ul + 1) * B] = hi
                llo[node, pl.ds(at, 32), ul * B : (ul + 1) * B] = lo


def fill_kernel(pos, l0, lu, ld, lhi, llo):
    y = pos[1]

    def step(node, _):
        fill(pos, lhi, llo, node, l0, node, y)
        fill(pos, lhi, llo, node, lu, node, (y + 3) & 3)
        fill(pos, lhi, llo, node, ld, node, (y + 1) & 3)
        return 0

    lax.fori_loop(0, 4, step, 0)


def product_kernel(first, *refs):
    if first:
        (pos, slots, lhi_in, llo_in, lf1, lf2, own, own_c, side, side_c,
         o0, o1, o2, o3, lhi, llo, selhi, sello) = refs
        outs = ((2, o2), (1, o1), (3, o3), (0, o0))
        pieces = ((own,), (own_c,), (side,), (side_c,))
    else:
        (pos, slots, lhi, llo, top, bot, top_c, bot_c, side, side_c,
         o0, o1, o2, o3, selhi, sello) = refs
        outs = ((2, o2), (1, o1), (3, o3), (0, o0))
        pieces = ((top, bot), (top_c, bot_c), (side,), (side_c,))
    h, y, xl, z, core = pos[0], pos[1], pos[2], pos[3], pos[4]
    at_half = (xl, xl, 1 - xl, 1 - xl)
    at_pair = (core, 1 - core, core, 1 - core)

    if first:

        def fill_far(i, _):
            fill(pos, lhi, llo, i, lf1, i, (y + 2) & 3)
            fill(pos, lhi, llo, i + 2, lf2, i, (y + 2) & 3)
            return 0

        lax.fori_loop(0, 2, fill_far, 0)

    m0 = 16 * (h if first else 1 - h) + 4 * y
    for k, (i, dst) in enumerate(outs):
        node = (z + i) & 3
        for m in range(4):
            cm = slots[node, m0 + m] & 7
            for p in range(4):
                for b in range(2):
                    ck = slots[node, 16 * at_half[p] + 4 * z + 2 * at_pair[p] + b] & 3
                    lanes = pl.ds(pl.multiple_of(ck * B, B), B)
                    if len(pieces[p]) == 1:
                        blk = pieces[p][0][pl.ds(pl.multiple_of(cm * B, B), B), lanes]
                    else:
                        sub = pl.ds(pl.multiple_of((cm & 3) * B, B), B)
                        blk = jnp.where(cm < 4, pieces[p][0][sub, lanes], pieces[p][1][sub, lanes])
                    hi, lo = split(blk)
                    e = p * 2 + b
                    selhi[k & 1, m * B : (m + 1) * B, e * B : (e + 1) * B] = hi
                    sello[k & 1, m * B : (m + 1) * B, e * B : (e + 1) * B] = lo
        bh = lhi[node]
        bl = llo[node]
        ah = selhi[k & 1]
        dst[...] = dot(ah, bh) + (dot(ah, bl) + dot(sello[k & 1], bh))


def product(first, *args):
    out = [shape(512, 256)] * 4
    if first:
        out = out + [jax.ShapeDtypeStruct((4, 1024, 256), bf16)] * 2
    return call(
        lambda *refs: product_kernel(first, *refs),
        out,
        [smem] * 2 + [vmem] * (len(args) - 2),
        [vmem] * len(out),
        [pltpu.VMEM((2, 512, 1024), bf16), pltpu.VMEM((2, 512, 1024), bf16)],
        mib=14,
        cost=24 * MIB,
        name="product_own" if first else "product_far",
        alias={2: 4, 3: 5} if first else {},
    )(*args)


def half_rows(h, y, rows, buf):
    for e in range(4):
        for i, src in enumerate(rows):
            to = pl.multiple_of(e * B + ((y - i) & 3) * 32, 32)
            for ul in range(2):
                at = pl.multiple_of(((h * 4 + e) * 2 + ul) * 32, 32)
                buf[pl.ds(to, 32), ul * B : (ul + 1) * B] = src[pl.ds(at, 32), :]
    return buf[...]


def far_kernel(o0, q1, q2, other):
    other[...] = -(o0[...] + (q1[...] + q2[...])).T


def prods_kernel(pos, n0, q1, q2, far, v0, v1, v2, v3, near, prods, buf):
    h, y = pos[0], pos[1]
    rows = (v0, v1, v2, v3)
    t = -(n0[...] + (q1[...] + q2[...])).T
    near[...] = t
    s = dot3(t, half_rows(h, y, rows, buf))
    s = s + dot3(far[...], half_rows(1 - h, y, rows, buf))
    prods[0] = s[:B, :B]
    prods[1] = s[:B, B:]
    prods[2] = s[B:, B:]


def rows_kernel(pos, place, slot, ulen, llen, mine, other, parent, up, low):
    h, y = pos[0], pos[1]
    r = h * 4 + y
    up[...] = jnp.zeros_like(up)
    low[...] = jnp.zeros_like(low)
    for k, src in ((0, mine), (1, other)):
        node = h if k == 0 else 1 - h
        lp = parent[node].T
        for e in range(4):
            p = place[node, 4 * r + e]
            at = pl.multiple_of((slot[node, 4 * r + e] & 7) * B, B)
            gu = jnp.where(p < ulen[node], src[:B, e * B : (e + 1) * B], 0.0)
            gl = src[B:, e * B : (e + 1) * B] - dot3(lp, gu)
            gl = jnp.where(p < llen[node], gl, 0.0)
            up[node, :, pl.ds(at, B)] = gu
            low[node, :, pl.ds(at, B)] = gl


def diag_kernel(pos, mine, other, uinv, linv, parent, du, pr, dl):
    h = pos[0]
    for k, src in ((0, mine), (1, other)):
        node = h if k == 0 else 1 - h
        lp = parent[node]
        lpt = lp.T
        cross = src[1]
        d = uinv[node] - src[0].T
        row = -(dot3(d, lp) + cross)
        low = src[2].T - dot3(cross.T, lp)
        du[node] = d
        pr[node] = row
        dl[node] = linv[node] - dot3(lpt, row) - low


def call(kernel, out_shape, in_specs, out_specs, scratch=(), mib=16, name=None, alias={}, cost=None):
    return pl.pallas_call(
        kernel,
        out_shape=out_shape,
        in_specs=in_specs,
        out_specs=out_specs,
        scratch_shapes=list(scratch),
        compiler_params=params(mib),
        name=name,
        input_output_aliases=alias,
        cost_estimate=pl.CostEstimate(flops=0, transcendentals=0, bytes_accessed=cost) if cost else None,
    )


def shape(*s):
    return jax.ShapeDtypeStruct(s, f32)


def body(
    ainv_top,
    block_owner,
    upper_list,
    upper_len,
    upper_panel,
    upper_dinv,
    lower_len,
    lower_panel,
    lower_parent,
    lower_dinv,
):
    pos = jnp.stack([lax.axis_index(n) for n in ("xh", "y", "xl", "z", "core")]).astype(jnp.int32)
    pp = lax.ppermute
    mirror = [(0, 3), (1, 2), (2, 1), (3, 0)]
    ints = jax.ShapeDtypeStruct((2, 32), jnp.int32)
    place, slot = call(
        sort_kernel, [ints] * 2, [smem] * 2, [smem] * 2, [pltpu.SMEM((64,), jnp.int32)], name="sort"
    )(block_owner, upper_list)
    sliced = call(
        slice_kernel, shape(8, 2, 4, 32, B), [hbm] * 2, hbm, [pltpu.SemaphoreType.DMA], name="slices"
    )(upper_panel.reshape(2, 4, B, B), lower_panel.reshape(2, 4, B, B))
    got = swap_all(sliced.reshape(8, 256, B), ROW)
    a = ainv_top
    a_nr = pp(a, "xl", shift(2, 1))
    a_fr = pp(a, RING, mirror)
    a_co = pp(a, "core", shift(2, 1))
    got, a_co = lax.optimization_barrier((got, a_co))
    ordered, v0, v1, v2, v3 = call(
        order_kernel,
        [pltpu.HBM((4, 520, B), f32)] + [pltpu.HBM((512, B), f32)] * 4,
        [smem] * 5 + [vmem],
        [hbm] * 5,
        [pltpu.VMEM((4, 520, B), f32), pltpu.SemaphoreType.DMA((8,))],
        name="order",
    )(pos, place, slot, upper_len, lower_len, got)
    l0 = swap_all(ordered, "z")
    v1, v2, v3 = (pp(v, "y", shift(4, i + 1)) for i, v in enumerate((v1, v2, v3)))
    l0, v1, v2, v3 = lax.optimization_barrier((l0, v1, v2, v3))
    lu = pp(l0, "y", shift(4, 1))
    ld = pp(l0, "y", shift(4, 3))
    slots = l0[:, 512, :32].astype(jnp.int32)
    a_f1 = pp(a_nr[:512], RING, mirror)
    a_f2 = pp(a_fr[512:], "xl", shift(2, 1))
    a_nr, a_fr, lu, ld = lax.optimization_barrier((a_nr, a_fr, lu, ld))
    c_nr = pp(a_nr, "core", shift(2, 1))
    lf1 = pp(lu[:2], "y", shift(4, 1))
    lf2 = pp(ld[2:], "y", shift(4, 3))
    k_fr, lf1, lf2 = lax.optimization_barrier((a_fr, lf1, lf2))
    c_fr = pp(k_fr, "core", shift(2, 1))
    lf1, lf2, a_f1, a_f2 = lax.optimization_barrier((lf1, lf2, a_f1, a_f2))
    parts = jax.ShapeDtypeStruct((4, 1024, 256), bf16)
    hi, lo = call(fill_kernel, [parts] * 2, [smem] + [vmem] * 3, [vmem] * 2, mib=14, cost=12 * MIB, name="fill")(
        pos, l0, lu, ld
    )
    a_f1, a_f2, hi, lo = lax.optimization_barrier((a_f1, a_f2, hi, lo))
    c_f1 = pp(a_f1, "core", shift(2, 1))
    c_f2 = pp(a_f2, "core", shift(2, 1))
    n0, n1, n2, n3, hi, lo = product(True, pos, slots, hi, lo, lf1, lf2, a, a_co, a_nr, c_nr)
    ra = pp(n2, "z", shift(4, 1))
    q3 = pp(n3, "z", shift(4, 3))
    o0, o1, o2, o3 = product(False, pos, slots, hi, lo, a_f1, a_f2, c_f1, c_f2, a_fr, c_fr)
    o1, ra = lax.optimization_barrier((o1, ra))
    o2, q3 = lax.optimization_barrier((o2, q3))
    q1 = pp(o1, "z", shift(4, 1))
    rb = pp(o2, "z", shift(4, 3))
    near_up = pp(n1 + ra, "z", shift(4, 1))
    far_dn = pp(o3 + rb, "z", shift(4, 3))
    far = call(far_kernel, shape(256, 512), [vmem] * 3, vmem, mib=8, name="far")(o0, q1, far_dn)
    mine, prods = call(
        prods_kernel,
        [shape(256, 512), shape(3, B, B)],
        [smem] + [vmem] * 8,
        [vmem] * 2,
        [pltpu.VMEM((512, 256), f32)],
        mib=16,
        name="prods",
    )(pos, n0, near_up, q3, far, v0, v1, v2, v3)
    s1 = pp(prods, "y", shift(4, 1))
    s2 = pp(prods, "y", shift(4, 2))
    s3 = pp(prods, "y", shift(4, 3))
    other = pp(far, "xh", shift(2, 1))
    mine_sum = (prods + s1) + (s2 + s3)
    other_sum = pp(mine_sum, "xh", shift(2, 1))
    upper_rows, lower_rows = call(
        rows_kernel, [shape(2, B, 1024)] * 2, [smem] * 5 + [vmem] * 3, [vmem] * 2, name="rows"
    )(pos, place, slot, upper_len, lower_len, mine, other, lower_parent)
    other_sum, upper_rows = lax.optimization_barrier((other_sum, upper_rows))
    diag_up, parent_row, diag_low = call(
        diag_kernel, [shape(2, B, B)] * 3, [smem] + [vmem] * 5, [vmem] * 3, name="diag"
    )(pos, mine_sum, other_sum, upper_dinv, lower_dinv, lower_parent)
    return (upper_rows, diag_up, lower_rows, parent_row, diag_low)


def solution(mesh):
    fine = Mesh(mesh.devices.reshape(2, 4, 2, 4, 2), ("xh", "y", "xl", "z", "core"))
    row = ("xh", "y")
    col = ("xl", "z", "core")
    in_specs = (
        P(row, col),
        P(),
        P(col, None),
        P(col),
        P(col, row, None),
        P(col, None, None),
        P(col),
        P(col, row, None),
        P(col, None, None),
        P(col, None, None),
    )
    out_specs = (
        P(col, None, row),
        P(col, None, None),
        P(col, None, row),
        P(col, None, None),
        P(col, None, None),
    )
    return jax.shard_map(body, mesh=fine, in_specs=in_specs, out_specs=out_specs, check_vma=False)
```

```python
import jax
import jax.numpy as jnp
from jax import lax
from jax.experimental import pallas as pl
from jax.experimental.pallas import tpu as pltpu
from jax.sharding import Mesh, PartitionSpec as P

B = 128
MIB = 1 << 20
ROW = ("xh", "y")
RING = ("xh", "xl")
f32 = jnp.float32
bf16 = jnp.bfloat16

smem = pl.BlockSpec(memory_space=pltpu.SMEM)
vmem = pl.BlockSpec(memory_space=pltpu.VMEM)
hbm = pl.BlockSpec(memory_space=pltpu.HBM)


def params(mib):
    return pltpu.CompilerParams(vmem_limit_bytes=mib * MIB)


def shift(n, s):
    return [(i, (i + s) % n) for i in range(n)]


def swap_all(x, axis):
    return lax.all_to_all(x, axis, split_axis=0, concat_axis=0, tiled=True)


def split(x):
    hi = x.astype(bf16)
    return hi, (x - hi.astype(f32)).astype(bf16)


def dot(a, b):
    return jnp.dot(a, b, preferred_element_type=f32)


def dot3(a, b):
    ah, al = split(a)
    bh, bl = split(b)
    return dot(ah, bh) + (dot(ah, bl) + dot(al, bh))


def sort_kernel(owner, names, place, slot, inv):
    for node in range(2):

        def clear(t, _):
            inv[t] = -1
            return 0

        def mark(q, _):
            inv[owner[names[node, q]]] = q
            return 0

        def pick(g, _):
            t = 4 * g
            lo = jnp.where(inv[t] >= 0, 0, jnp.where(inv[t + 1] >= 0, 1, 2))
            hi = jnp.where(inv[t + 3] >= 0, 3, jnp.where(inv[t + 2] >= 0, 2, 1))
            place[node, 2 * g] = inv[t + lo]
            slot[node, 2 * g] = t + lo
            place[node, 2 * g + 1] = inv[t + hi]
            slot[node, 2 * g + 1] = t + hi
            return 0

        lax.fori_loop(0, 64, clear, 0)
        lax.fori_loop(0, 32, mark, 0)
        lax.fori_loop(0, 16, pick, 0)


def slice_kernel(up, low, out, sem):
    copies = []
    for node in range(2):
        for q in range(4):
            for ul, src in enumerate((up, low)):
                copies.append(
                    pltpu.make_async_copy(src.at[node, :, q * 32 : (q + 1) * 32, :], out.at[node * 4 + q, ul], sem)
                )
    for c in copies:
        c.start()
    for c in copies:
        c.wait()


def order_kernel(pos, place, slot, ulen, llen, got, out, v0, v1, v2, v3, buf, sems):
    node, y = pos[0], pos[1]
    lens = (ulen[node], llen[node])
    lane = lax.broadcasted_iota(jnp.int32, (8, B), 1)
    info = jnp.zeros((8, B), f32)
    for s in range(32):
        info = jnp.where(lane == s, slot[node, s].astype(f32), info)
    copies = []
    for q in range(4):
        for h in range(2):
            for e in range(4):
                p = place[node, 16 * h + 4 * q + e]
                for ul in range(2):
                    at = pl.multiple_of((ul * 4 + (p & 3)) * 32, 32)
                    v = got[p >> 2, pl.ds(at, 32), :]
                    v = jnp.where(p < lens[ul], v, 0.0)
                    row = ((h * 4 + e) * 2 + ul) * 32
                    buf[q, row : row + 32, :] = v
        buf[q, 512:520, :] = info
        copies.append(pltpu.make_async_copy(buf.at[q], out.at[q], sems.at[q]))
        copies[-1].start()
    for i, v in enumerate((v0, v1, v2, v3)):
        copies.append(pltpu.make_async_copy(buf.at[(y + i) & 3, :512], v, sems.at[4 + i]))
        copies[-1].start()
    for c in copies:
        c.wait()


def fill(pos, lhi, llo, node, src, row, ys):
    xl, core = pos[2], pos[4]
    for p in range(4):
        half = xl if p < 2 else 1 - xl
        pair = core if p % 2 == 0 else 1 - core
        for b in range(2):
            e = half * 4 + pair * 2 + b
            for ul in range(2):
                r = pl.multiple_of((e * 2 + ul) * 32, 32)
                hi, lo = split(src[row, pl.ds(r, 32), :])
                at = pl.multiple_of((p * 2 + b) * B + ys * 32, 32)
                lhi[node, pl.ds(at, 32), ul * B : (ul + 1) * B] = hi
                llo[node, pl.ds(at, 32), ul * B : (ul + 1) * B] = lo


def fill_kernel(pos, l0, lu, ld, lhi, llo):
    y = pos[1]

    def step(node, _):
        fill(pos, lhi, llo, node, l0, node, y)
        fill(pos, lhi, llo, node, lu, node, (y + 3) & 3)
        fill(pos, lhi, llo, node, ld, node, (y + 1) & 3)
        return 0

    lax.fori_loop(0, 4, step, 0)


def product_kernel(first, *refs):
    if first:
        (pos, slots, lhi_in, llo_in, lf1, lf2, own, own_c, side, side_c,
         o0, o1, o2, o3, lhi, llo, selhi, sello) = refs
        outs = ((2, o2), (1, o1), (3, o3), (0, o0))
        pieces = ((own,), (own_c,), (side,), (side_c,))
    else:
        (pos, slots, lhi, llo, top, bot, top_c, bot_c, side, side_c,
         o0, o1, o2, o3, selhi, sello) = refs
        outs = ((2, o2), (1, o1), (3, o3), (0, o0))
        pieces = ((top, bot), (top_c, bot_c), (side,), (side_c,))
    h, y, xl, z, core = pos[0], pos[1], pos[2], pos[3], pos[4]
    at_half = (xl, xl, 1 - xl, 1 - xl)
    at_pair = (core, 1 - core, core, 1 - core)

    if first:

        def fill_far(i, _):
            fill(pos, lhi, llo, i, lf1, i, (y + 2) & 3)
            fill(pos, lhi, llo, i + 2, lf2, i, (y + 2) & 3)
            return 0

        lax.fori_loop(0, 2, fill_far, 0)

    m0 = 16 * (h if first else 1 - h) + 4 * y
    for k, (i, dst) in enumerate(outs):
        node = (z + i) & 3
        for m in range(4):
            cm = slots[node, m0 + m] & 7
            for p in range(4):
                for b in range(2):
                    ck = slots[node, 16 * at_half[p] + 4 * z + 2 * at_pair[p] + b] & 3
                    lanes = pl.ds(pl.multiple_of(ck * B, B), B)
                    if len(pieces[p]) == 1:
                        blk = pieces[p][0][pl.ds(pl.multiple_of(cm * B, B), B), lanes]
                    else:
                        sub = pl.ds(pl.multiple_of((cm & 3) * B, B), B)
                        blk = jnp.where(cm < 4, pieces[p][0][sub, lanes], pieces[p][1][sub, lanes])
                    hi, lo = split(blk)
                    e = p * 2 + b
                    selhi[k & 1, m * B : (m + 1) * B, e * B : (e + 1) * B] = hi
                    sello[k & 1, m * B : (m + 1) * B, e * B : (e + 1) * B] = lo
        bh = lhi[node]
        bl = llo[node]
        ah = selhi[k & 1]
        dst[...] = dot(ah, bh) + (dot(ah, bl) + dot(sello[k & 1], bh))


def product(first, *args):
    out = [shape(512, 256)] * 4
    if first:
        out = out + [jax.ShapeDtypeStruct((4, 1024, 256), bf16)] * 2
    return call(
        lambda *refs: product_kernel(first, *refs),
        out,
        [smem] * 2 + [vmem] * (len(args) - 2),
        [vmem] * len(out),
        [pltpu.VMEM((2, 512, 1024), bf16), pltpu.VMEM((2, 512, 1024), bf16)],
        mib=14,
        name="product_own" if first else "product_far",
        alias={2: 4, 3: 5} if first else {},
    )(*args)


def half_rows(h, y, rows, buf):
    for e in range(4):
        for i, src in enumerate(rows):
            to = pl.multiple_of(e * B + ((y - i) & 3) * 32, 32)
            for ul in range(2):
                at = pl.multiple_of(((h * 4 + e) * 2 + ul) * 32, 32)
                buf[pl.ds(to, 32), ul * B : (ul + 1) * B] = src[pl.ds(at, 32), :]
    return buf[...]


def far_kernel(o0, q1, q2, up, low):
    t = -(o0[...] + (q1[...] + q2[...])).T
    up[...] = t[:B]
    low[...] = t[B:]


def prods_kernel(pos, n0, q1, q2, up, low, v0, v1, v2, v3, near, prods, buf):
    h, y = pos[0], pos[1]
    rows = (v0, v1, v2, v3)
    t = -(n0[...] + (q1[...] + q2[...])).T
    near[...] = t
    s = dot3(t, half_rows(h, y, rows, buf))
    s = s + dot3(jnp.concatenate([up[...], low[...]], axis=0), half_rows(1 - h, y, rows, buf))
    prods[0] = s[:B, :B]
    prods[1] = s[:B, B:]
    prods[2] = s[B:, B:]


def rows_kernel(pos, place, slot, ulen, llen, mine, other_up, other_low, parent, up, low):
    h, y = pos[0], pos[1]
    r = h * 4 + y
    up[...] = jnp.zeros_like(up)
    low[...] = jnp.zeros_like(low)
    for k, src_up, src_low in ((0, mine.at[:B], mine.at[B:]), (1, other_up, other_low)):
        node = h if k == 0 else 1 - h
        lp = parent[node].T
        for e in range(4):
            p = place[node, 4 * r + e]
            at = pl.multiple_of((slot[node, 4 * r + e] & 7) * B, B)
            gu = jnp.where(p < ulen[node], src_up[:, e * B : (e + 1) * B], 0.0)
            gl = src_low[:, e * B : (e + 1) * B] - dot3(lp, gu)
            gl = jnp.where(p < llen[node], gl, 0.0)
            up[node, :, pl.ds(at, B)] = gu
            low[node, :, pl.ds(at, B)] = gl


def diag_kernel(pos, mine, other, uinv, linv, parent, du, pr, dl):
    h = pos[0]
    for k, src in ((0, mine), (1, other)):
        node = h if k == 0 else 1 - h
        lp = parent[node]
        lpt = lp.T
        cross = src[1]
        d = uinv[node] - src[0].T
        row = -(dot3(d, lp) + cross)
        low = src[2].T - dot3(cross.T, lp)
        du[node] = d
        pr[node] = row
        dl[node] = linv[node] - dot3(lpt, row) - low


def call(kernel, out_shape, in_specs, out_specs, scratch=(), mib=16, name=None, alias={}):
    return pl.pallas_call(
        kernel,
        out_shape=out_shape,
        in_specs=in_specs,
        out_specs=out_specs,
        scratch_shapes=list(scratch),
        compiler_params=params(mib),
        name=name,
        input_output_aliases=alias,
    )


def shape(*s):
    return jax.ShapeDtypeStruct(s, f32)


def body(
    ainv_top,
    block_owner,
    upper_list,
    upper_len,
    upper_panel,
    upper_dinv,
    lower_len,
    lower_panel,
    lower_parent,
    lower_dinv,
):
    pos = jnp.stack([lax.axis_index(n) for n in ("xh", "y", "xl", "z", "core")]).astype(jnp.int32)
    pp = lax.ppermute
    mirror = [(0, 3), (1, 2), (2, 1), (3, 0)]
    ints = jax.ShapeDtypeStruct((2, 32), jnp.int32)
    place, slot = call(
        sort_kernel, [ints] * 2, [smem] * 2, [smem] * 2, [pltpu.SMEM((64,), jnp.int32)], name="sort"
    )(block_owner, upper_list)
    sliced = call(
        slice_kernel, pltpu.HBM((8, 2, 4, 32, B), f32), [hbm] * 2, hbm, [pltpu.SemaphoreType.DMA], name="slices"
    )(upper_panel.reshape(2, 4, B, B), lower_panel.reshape(2, 4, B, B))
    got = swap_all(sliced.reshape(8, 256, B), ROW)
    a = ainv_top
    a_nr = pp(a, "xl", shift(2, 1))
    a_fr = pp(a, RING, mirror)
    a_co = pp(a, "core", shift(2, 1))
    got, a_co = lax.optimization_barrier((got, a_co))
    ordered, v0, v1, v2, v3 = call(
        order_kernel,
        [pltpu.HBM((4, 520, B), f32)] + [pltpu.HBM((512, B), f32)] * 4,
        [smem] * 5 + [vmem],
        [hbm] * 5,
        [pltpu.VMEM((4, 520, B), f32), pltpu.SemaphoreType.DMA((8,))],
        name="order",
    )(pos, place, slot, upper_len, lower_len, got)
    l0 = swap_all(ordered, "z")
    v1, v2, v3 = (pp(v, "y", shift(4, i + 1)) for i, v in enumerate((v1, v2, v3)))
    l0, v1, v2, v3 = lax.optimization_barrier((l0, v1, v2, v3))
    lu = pp(l0, "y", shift(4, 1))
    ld = pp(l0, "y", shift(4, 3))
    a_f1 = pp(a_nr[:512], RING, mirror)
    a_f2 = pp(a_fr[512:], "xl", shift(2, 1))
    lf1 = pp(lu[:2], "y", shift(4, 1))
    lf2 = pp(ld[2:], "y", shift(4, 3))
    k_nr, _, _ = lax.optimization_barrier((a_nr, lf1, lf2))
    c_nr = pp(k_nr, "core", shift(2, 1))
    parts = jax.ShapeDtypeStruct((4, 1024, 256), bf16)
    hi, lo = call(fill_kernel, [parts] * 2, [smem] + [vmem] * 3, [vmem] * 2, mib=14, name="fill")(
        pos, l0, lu, ld
    )
    a_f1, a_f2, hi, lo = lax.optimization_barrier((a_f1, a_f2, hi, lo))
    c_f1 = pp(a_f1, "core", shift(2, 1))
    c_f2 = pp(a_f2, "core", shift(2, 1))
    info, c_f1, c_f2 = lax.optimization_barrier((l0, c_f1, c_f2))
    slots = info[:, 512, :32].astype(jnp.int32)
    k_fr, c_f1, c_f2 = lax.optimization_barrier((a_fr, c_f1, c_f2))
    c_fr = pp(k_fr, "core", shift(2, 1))
    n0, n1, n2, n3, hi, lo = product(True, pos, slots, hi, lo, lf1, lf2, a, a_co, a_nr, c_nr)
    ra = pp(n2, "z", shift(4, 1))
    q3 = pp(n3, "z", shift(4, 3))
    o0, o1, o2, o3 = product(False, pos, slots, hi, lo, a_f1, a_f2, c_f1, c_f2, a_fr, c_fr)
    o1, ra = lax.optimization_barrier((o1, ra))
    o2, q3 = lax.optimization_barrier((o2, q3))
    q1 = pp(o1, "z", shift(4, 1))
    rb = pp(o2, "z", shift(4, 3))
    near_up = pp(n1 + ra, "z", shift(4, 1))
    far_dn = pp(o3 + rb, "z", shift(4, 3))
    far_up, far_low = call(far_kernel, [shape(B, 512)] * 2, [vmem] * 3, [vmem] * 2, mib=8, name="far")(o0, q1, far_dn)
    mine, prods = call(
        prods_kernel,
        [shape(256, 512), shape(3, B, B)],
        [smem] + [vmem] * 9,
        [vmem] * 2,
        [pltpu.VMEM((512, 256), f32)],
        mib=16,
        name="prods",
    )(pos, n0, near_up, q3, far_up, far_low, v0, v1, v2, v3)
    s1 = pp(prods, "y", shift(4, 1))
    s2 = pp(prods, "y", shift(4, 2))
    s3 = pp(prods, "y", shift(4, 3))
    other_up = pp(far_up, "xh", shift(2, 1))
    far_low, other_up = lax.optimization_barrier((far_low, other_up))
    other_low = pp(far_low, "xh", shift(2, 1))
    mine_sum = (prods + s1) + (s2 + s3)
    other_sum = pp(mine_sum, "xh", shift(2, 1))
    upper_rows, lower_rows = call(
        rows_kernel, [shape(2, B, 1024)] * 2, [smem] * 5 + [vmem] * 4, [vmem] * 2, name="rows"
    )(pos, place, slot, upper_len, lower_len, mine, other_up, other_low, lower_parent)
    other_sum, upper_rows = lax.optimization_barrier((other_sum, upper_rows))
    diag_up, parent_row, diag_low = call(
        diag_kernel, [shape(2, B, B)] * 3, [smem] + [vmem] * 5, [vmem] * 3, name="diag"
    )(pos, mine_sum, other_sum, upper_dinv, lower_dinv, lower_parent)
    return (upper_rows, diag_up, lower_rows, parent_row, diag_low)


def solution(mesh):
    fine = Mesh(mesh.devices.reshape(2, 4, 2, 4, 2), ("xh", "y", "xl", "z", "core"))
    row = ("xh", "y")
    col = ("xl", "z", "core")
    in_specs = (
        P(row, col),
        P(),
        P(col, None),
        P(col),
        P(col, row, None),
        P(col, None, None),
        P(col),
        P(col, row, None),
        P(col, None, None),
        P(col, None, None),
    )
    out_specs = (
        P(col, None, row),
        P(col, None, None),
        P(col, None, row),
        P(col, None, None),
        P(col, None, None),
    )
    return jax.shard_map(body, mesh=fine, in_specs=in_specs, out_specs=out_specs, check_vma=False)
```

```python
import jax
import jax.numpy as jnp
from jax import lax
from jax.experimental import pallas as pl
from jax.experimental.pallas import tpu as pltpu
from jax.sharding import Mesh, PartitionSpec as P

B = 128
MIB = 1 << 20
ROW = ("xh", "y")
RING = ("xh", "xl")
f32 = jnp.float32
bf16 = jnp.bfloat16

smem = pl.BlockSpec(memory_space=pltpu.SMEM)
vmem = pl.BlockSpec(memory_space=pltpu.VMEM)
hbm = pl.BlockSpec(memory_space=pltpu.HBM)


def params(mib):
    return pltpu.CompilerParams(vmem_limit_bytes=mib * MIB)


def shift(n, s):
    return [(i, (i + s) % n) for i in range(n)]


def swap_all(x, axis):
    return lax.all_to_all(x, axis, split_axis=0, concat_axis=0, tiled=True)


def split(x):
    hi = x.astype(bf16)
    return hi, (x - hi.astype(f32)).astype(bf16)


def dot(a, b):
    return jnp.dot(a, b, preferred_element_type=f32)


def dot3(a, b):
    ah, al = split(a)
    bh, bl = split(b)
    return dot(ah, bh) + (dot(ah, bl) + dot(al, bh))


def sort_kernel(owner, names, place, slot, inv):
    for node in range(2):

        def clear(t, _):
            inv[t] = -1
            return 0

        def mark(q, _):
            inv[owner[names[node, q]]] = q
            return 0

        def pick(g, _):
            t = 4 * g
            lo = jnp.where(inv[t] >= 0, 0, jnp.where(inv[t + 1] >= 0, 1, 2))
            hi = jnp.where(inv[t + 3] >= 0, 3, jnp.where(inv[t + 2] >= 0, 2, 1))
            place[node, 2 * g] = inv[t + lo]
            slot[node, 2 * g] = t + lo
            place[node, 2 * g + 1] = inv[t + hi]
            slot[node, 2 * g + 1] = t + hi
            return 0

        lax.fori_loop(0, 64, clear, 0)
        lax.fori_loop(0, 32, mark, 0)
        lax.fori_loop(0, 16, pick, 0)


def slice_kernel(up, low, out, sem):
    copies = []
    for node in range(2):
        for q in range(4):
            for ul, src in enumerate((up, low)):
                copies.append(
                    pltpu.make_async_copy(src.at[node, :, q * 32 : (q + 1) * 32, :], out.at[node * 4 + q, ul], sem)
                )
    for c in copies:
        c.start()
    for c in copies:
        c.wait()


def order_kernel(pos, place, slot, ulen, llen, got, out, v0, v1, v2, v3, buf, sems):
    node, y = pos[0], pos[1]
    lens = (ulen[node], llen[node])
    lane = lax.broadcasted_iota(jnp.int32, (8, B), 1)
    info = jnp.zeros((8, B), f32)
    for s in range(32):
        info = jnp.where(lane == s, slot[node, s].astype(f32), info)
    copies = []
    for q in range(4):
        for h in range(2):
            for e in range(4):
                p = place[node, 16 * h + 4 * q + e]
                for ul in range(2):
                    at = pl.multiple_of((ul * 4 + (p & 3)) * 32, 32)
                    v = got[p >> 2, pl.ds(at, 32), :]
                    v = jnp.where(p < lens[ul], v, 0.0)
                    row = ((h * 4 + e) * 2 + ul) * 32
                    buf[q, row : row + 32, :] = v
        buf[q, 512:520, :] = info
        copies.append(pltpu.make_async_copy(buf.at[q], out.at[q], sems.at[q]))
        copies[-1].start()
    for i, v in enumerate((v0, v1, v2, v3)):
        copies.append(pltpu.make_async_copy(buf.at[(y + i) & 3, :512], v, sems.at[4 + i]))
        copies[-1].start()
    for c in copies:
        c.wait()


def fill(pos, lhi, llo, node, src, row, ys):
    xl, core = pos[2], pos[4]
    for p in range(4):
        half = xl if p < 2 else 1 - xl
        pair = core if p % 2 == 0 else 1 - core
        for b in range(2):
            e = half * 4 + pair * 2 + b
            for ul in range(2):
                r = pl.multiple_of((e * 2 + ul) * 32, 32)
                hi, lo = split(src[row, pl.ds(r, 32), :])
                at = pl.multiple_of((p * 2 + b) * B + ys * 32, 32)
                lhi[node, pl.ds(at, 32), ul * B : (ul + 1) * B] = hi
                llo[node, pl.ds(at, 32), ul * B : (ul + 1) * B] = lo


def fill_kernel(pos, l0, lu, ld, lhi, llo):
    y = pos[1]

    def step(node, _):
        fill(pos, lhi, llo, node, l0, node, y)
        fill(pos, lhi, llo, node, lu, node, (y + 3) & 3)
        fill(pos, lhi, llo, node, ld, node, (y + 1) & 3)
        return 0

    lax.fori_loop(0, 4, step, 0)


def product_kernel(first, *refs):
    if first:
        (pos, slots, lhi_in, llo_in, lf1, lf2, own, own_c, side, side_c,
         o0, o1, o2, o3, lhi, llo, selhi, sello) = refs
        outs = ((2, o2), (1, o1), (3, o3), (0, o0))
        pieces = ((own,), (own_c,), (side,), (side_c,))
    else:
        (pos, slots, lhi, llo, top, bot, top_c, bot_c, side, side_c,
         o0, o1, o2, o3, selhi, sello) = refs
        outs = ((2, o2), (1, o1), (3, o3), (0, o0))
        pieces = ((top, bot), (top_c, bot_c), (side,), (side_c,))
    h, y, xl, z, core = pos[0], pos[1], pos[2], pos[3], pos[4]
    at_half = (xl, xl, 1 - xl, 1 - xl)
    at_pair = (core, 1 - core, core, 1 - core)

    if first:

        def fill_far(i, _):
            fill(pos, lhi, llo, i, lf1, i, (y + 2) & 3)
            fill(pos, lhi, llo, i + 2, lf2, i, (y + 2) & 3)
            return 0

        lax.fori_loop(0, 2, fill_far, 0)

    m0 = 16 * (h if first else 1 - h) + 4 * y
    for k, (i, dst) in enumerate(outs):
        node = (z + i) & 3
        for m in range(4):
            cm = slots[node, m0 + m] & 7
            for p in range(4):
                for b in range(2):
                    ck = slots[node, 16 * at_half[p] + 4 * z + 2 * at_pair[p] + b] & 3
                    lanes = pl.ds(pl.multiple_of(ck * B, B), B)
                    if len(pieces[p]) == 1:
                        blk = pieces[p][0][pl.ds(pl.multiple_of(cm * B, B), B), lanes]
                    else:
                        sub = pl.ds(pl.multiple_of((cm & 3) * B, B), B)
                        blk = jnp.where(cm < 4, pieces[p][0][sub, lanes], pieces[p][1][sub, lanes])
                    hi, lo = split(blk)
                    e = p * 2 + b
                    selhi[k & 1, m * B : (m + 1) * B, e * B : (e + 1) * B] = hi
                    sello[k & 1, m * B : (m + 1) * B, e * B : (e + 1) * B] = lo
        bh = lhi[node]
        bl = llo[node]
        ah = selhi[k & 1]
        dst[...] = dot(ah, bh) + (dot(ah, bl) + dot(sello[k & 1], bh))


def product(first, *args):
    out = [shape(512, 256)] * 4
    if first:
        out = out + [jax.ShapeDtypeStruct((4, 1024, 256), bf16)] * 2
    return call(
        lambda *refs: product_kernel(first, *refs),
        out,
        [smem] * 2 + [vmem] * (len(args) - 2),
        [vmem] * len(out),
        [pltpu.VMEM((2, 512, 1024), bf16), pltpu.VMEM((2, 512, 1024), bf16)],
        mib=14,
        name="product_own" if first else "product_far",
        alias={2: 4, 3: 5} if first else {},
    )(*args)


def half_rows(h, y, rows, buf):
    for e in range(4):
        for i, src in enumerate(rows):
            to = pl.multiple_of(e * B + ((y - i) & 3) * 32, 32)
            for ul in range(2):
                at = pl.multiple_of(((h * 4 + e) * 2 + ul) * 32, 32)
                buf[pl.ds(to, 32), ul * B : (ul + 1) * B] = src[pl.ds(at, 32), :]
    return buf[...]


def far_kernel(o0, q1, q2, up, low):
    t = -(o0[...] + (q1[...] + q2[...])).T
    up[...] = t[:B]
    low[...] = t[B:]


def prods_kernel(pos, n0, q1, q2, up, low, v0, v1, v2, v3, near, prods, buf):
    h, y = pos[0], pos[1]
    rows = (v0, v1, v2, v3)
    t = -(n0[...] + (q1[...] + q2[...])).T
    near[...] = t
    s = dot3(t, half_rows(h, y, rows, buf))
    s = s + dot3(jnp.concatenate([up[...], low[...]], axis=0), half_rows(1 - h, y, rows, buf))
    prods[0] = s[:B, :B]
    prods[1] = s[:B, B:]
    prods[2] = s[B:, B:]


def rows_kernel(pos, place, slot, ulen, llen, mine, other_up, other_low, parent, up, low):
    h, y = pos[0], pos[1]
    r = h * 4 + y
    up[...] = jnp.zeros_like(up)
    low[...] = jnp.zeros_like(low)
    for k, src_up, src_low in ((0, mine.at[:B], mine.at[B:]), (1, other_up, other_low)):
        node = h if k == 0 else 1 - h
        lp = parent[node].T
        for e in range(4):
            p = place[node, 4 * r + e]
            at = pl.multiple_of((slot[node, 4 * r + e] & 7) * B, B)
            gu = jnp.where(p < ulen[node], src_up[:, e * B : (e + 1) * B], 0.0)
            gl = src_low[:, e * B : (e + 1) * B] - dot3(lp, gu)
            gl = jnp.where(p < llen[node], gl, 0.0)
            up[node, :, pl.ds(at, B)] = gu
            low[node, :, pl.ds(at, B)] = gl


def diag_kernel(pos, mine, other, uinv, linv, parent, du, pr, dl):
    h = pos[0]
    for k, src in ((0, mine), (1, other)):
        node = h if k == 0 else 1 - h
        lp = parent[node]
        lpt = lp.T
        cross = src[1]
        d = uinv[node] - src[0].T
        row = -(dot3(d, lp) + cross)
        low = src[2].T - dot3(cross.T, lp)
        du[node] = d
        pr[node] = row
        dl[node] = linv[node] - dot3(lpt, row) - low


def call(kernel, out_shape, in_specs, out_specs, scratch=(), mib=16, name=None, alias={}):
    return pl.pallas_call(
        kernel,
        out_shape=out_shape,
        in_specs=in_specs,
        out_specs=out_specs,
        scratch_shapes=list(scratch),
        compiler_params=params(mib),
        name=name,
        input_output_aliases=alias,
    )


def shape(*s):
    return jax.ShapeDtypeStruct(s, f32)


def body(
    ainv_top,
    block_owner,
    upper_list,
    upper_len,
    upper_panel,
    upper_dinv,
    lower_len,
    lower_panel,
    lower_parent,
    lower_dinv,
):
    pos = jnp.stack([lax.axis_index(n) for n in ("xh", "y", "xl", "z", "core")]).astype(jnp.int32)
    pp = lax.ppermute
    mirror = [(0, 3), (1, 2), (2, 1), (3, 0)]
    ints = jax.ShapeDtypeStruct((2, 32), jnp.int32)
    place, slot = call(
        sort_kernel, [ints] * 2, [smem] * 2, [smem] * 2, [pltpu.SMEM((64,), jnp.int32)], name="sort"
    )(block_owner, upper_list)
    sliced = call(
        slice_kernel, pltpu.HBM((8, 2, 4, 32, B), f32), [hbm] * 2, hbm, [pltpu.SemaphoreType.DMA], name="slices"
    )(upper_panel.reshape(2, 4, B, B), lower_panel.reshape(2, 4, B, B))
    got = swap_all(sliced.reshape(8, 256, B), ROW)
    a = ainv_top
    a_nr = pp(a, "xl", shift(2, 1))
    a_fr = pp(a, RING, mirror)
    a_co = pp(a, "core", shift(2, 1))
    got, a_co = lax.optimization_barrier((got, a_co))
    ordered, v0, v1, v2, v3 = call(
        order_kernel,
        [pltpu.HBM((4, 520, B), f32)] + [pltpu.HBM((512, B), f32)] * 4,
        [smem] * 5 + [vmem],
        [hbm] * 5,
        [pltpu.VMEM((4, 520, B), f32), pltpu.SemaphoreType.DMA((8,))],
        name="order",
    )(pos, place, slot, upper_len, lower_len, got)
    l0 = swap_all(ordered, "z")
    v1, v2, v3 = (pp(v, "y", shift(4, i + 1)) for i, v in enumerate((v1, v2, v3)))
    l0, v1, v2, v3 = lax.optimization_barrier((l0, v1, v2, v3))
    lu = pp(l0, "y", shift(4, 1))
    ld = pp(l0, "y", shift(4, 3))
    a_f1 = pp(a_nr[:512], RING, mirror)
    a_f2 = pp(a_fr[512:], "xl", shift(2, 1))
    c_nr = pp(a_nr, "core", shift(2, 1))
    lf1 = pp(lu[:2], "y", shift(4, 1))
    lf2 = pp(ld[2:], "y", shift(4, 3))
    k_fr, lf1, lf2 = lax.optimization_barrier((a_fr, lf1, lf2))
    c_fr = pp(k_fr, "core", shift(2, 1))
    parts = jax.ShapeDtypeStruct((4, 1024, 256), bf16)
    hi, lo = call(fill_kernel, [parts] * 2, [smem] + [vmem] * 3, [vmem] * 2, mib=14, name="fill")(
        pos, l0, lu, ld
    )
    a_f1, a_f2, hi, lo = lax.optimization_barrier((a_f1, a_f2, hi, lo))
    c_f1 = pp(a_f1, "core", shift(2, 1))
    c_f2 = pp(a_f2, "core", shift(2, 1))
    info, c_f1, c_f2 = lax.optimization_barrier((l0, c_f1, c_f2))
    slots = info[:, 512, :32].astype(jnp.int32)
    n0, n1, n2, n3, hi, lo = product(True, pos, slots, hi, lo, lf1, lf2, a, a_co, a_nr, c_nr)
    ra = pp(n2, "z", shift(4, 1))
    q3 = pp(n3, "z", shift(4, 3))
    o0, o1, o2, o3 = product(False, pos, slots, hi, lo, a_f1, a_f2, c_f1, c_f2, a_fr, c_fr)
    o1, ra = lax.optimization_barrier((o1, ra))
    o2, q3 = lax.optimization_barrier((o2, q3))
    q1 = pp(o1, "z", shift(4, 1))
    rb = pp(o2, "z", shift(4, 3))
    near_up = pp(n1 + ra, "z", shift(4, 1))
    far_dn = pp(o3 + rb, "z", shift(4, 3))
    far_up, far_low = call(far_kernel, [shape(B, 512)] * 2, [vmem] * 3, [vmem] * 2, mib=8, name="far")(o0, q1, far_dn)
    mine, prods = call(
        prods_kernel,
        [shape(256, 512), shape(3, B, B)],
        [smem] + [vmem] * 9,
        [vmem] * 2,
        [pltpu.VMEM((512, 256), f32)],
        mib=16,
        name="prods",
    )(pos, n0, near_up, q3, far_up, far_low, v0, v1, v2, v3)
    s1 = pp(prods, "y", shift(4, 1))
    s2 = pp(prods, "y", shift(4, 2))
    s3 = pp(prods, "y", shift(4, 3))
    other_up = pp(far_up, "xh", shift(2, 1))
    far_low, other_up = lax.optimization_barrier((far_low, other_up))
    other_low = pp(far_low, "xh", shift(2, 1))
    mine_sum = (prods + s1) + (s2 + s3)
    other_sum = pp(mine_sum, "xh", shift(2, 1))
    upper_rows, lower_rows = call(
        rows_kernel, [shape(2, B, 1024)] * 2, [smem] * 5 + [vmem] * 4, [vmem] * 2, name="rows"
    )(pos, place, slot, upper_len, lower_len, mine, other_up, other_low, lower_parent)
    other_sum, upper_rows = lax.optimization_barrier((other_sum, upper_rows))
    diag_up, parent_row, diag_low = call(
        diag_kernel, [shape(2, B, B)] * 3, [smem] + [vmem] * 5, [vmem] * 3, name="diag"
    )(pos, mine_sum, other_sum, upper_dinv, lower_dinv, lower_parent)
    return (upper_rows, diag_up, lower_rows, parent_row, diag_low)


def solution(mesh):
    fine = Mesh(mesh.devices.reshape(2, 4, 2, 4, 2), ("xh", "y", "xl", "z", "core"))
    row = ("xh", "y")
    col = ("xl", "z", "core")
    in_specs = (
        P(row, col),
        P(),
        P(col, None),
        P(col),
        P(col, row, None),
        P(col, None, None),
        P(col),
        P(col, row, None),
        P(col, None, None),
        P(col, None, None),
    )
    out_specs = (
        P(col, None, row),
        P(col, None, None),
        P(col, None, row),
        P(col, None, None),
        P(col, None, None),
    )
    return jax.shard_map(body, mesh=fine, in_specs=in_specs, out_specs=out_specs, check_vma=False)
```

```python
import jax
import jax.numpy as jnp
from jax import lax
from jax.experimental import pallas as pl
from jax.experimental.pallas import tpu as pltpu
from jax.sharding import Mesh, PartitionSpec as P

B = 128
MIB = 1 << 20
ROW = ("xh", "y")
RING = ("xh", "xl")
f32 = jnp.float32
bf16 = jnp.bfloat16

smem = pl.BlockSpec(memory_space=pltpu.SMEM)
vmem = pl.BlockSpec(memory_space=pltpu.VMEM)
hbm = pl.BlockSpec(memory_space=pltpu.HBM)


def params(mib):
    return pltpu.CompilerParams(vmem_limit_bytes=mib * MIB)


def shift(n, s):
    return [(i, (i + s) % n) for i in range(n)]


def swap_all(x, axis):
    return lax.all_to_all(x, axis, split_axis=0, concat_axis=0, tiled=True)


def split(x):
    hi = x.astype(bf16)
    return hi, (x - hi.astype(f32)).astype(bf16)


def dot(a, b):
    return jnp.dot(a, b, preferred_element_type=f32)


def dot3(a, b):
    ah, al = split(a)
    bh, bl = split(b)
    return dot(ah, bh) + (dot(ah, bl) + dot(al, bh))


def sort_kernel(owner, names, place, slot, inv):
    for node in range(2):

        def clear(t, _):
            inv[t] = -1
            return 0

        def mark(q, _):
            inv[owner[names[node, q]]] = q
            return 0

        def pick(g, _):
            t = 4 * g
            lo = jnp.where(inv[t] >= 0, 0, jnp.where(inv[t + 1] >= 0, 1, 2))
            hi = jnp.where(inv[t + 3] >= 0, 3, jnp.where(inv[t + 2] >= 0, 2, 1))
            place[node, 2 * g] = inv[t + lo]
            slot[node, 2 * g] = t + lo
            place[node, 2 * g + 1] = inv[t + hi]
            slot[node, 2 * g + 1] = t + hi
            return 0

        lax.fori_loop(0, 64, clear, 0)
        lax.fori_loop(0, 32, mark, 0)
        lax.fori_loop(0, 16, pick, 0)


def slice_kernel(up, low, out, sem):
    copies = []
    for node in range(2):
        for q in range(4):
            for ul, src in enumerate((up, low)):
                copies.append(
                    pltpu.make_async_copy(src.at[node, :, q * 32 : (q + 1) * 32, :], out.at[node * 4 + q, ul], sem)
                )
    for c in copies:
        c.start()
    for c in copies:
        c.wait()


def order_kernel(pos, place, slot, ulen, llen, got, out, v0, v1, v2, v3, buf, sems):
    node, y = pos[0], pos[1]
    lens = (ulen[node], llen[node])
    lane = lax.broadcasted_iota(jnp.int32, (8, B), 1)
    info = jnp.zeros((8, B), f32)
    for s in range(32):
        info = jnp.where(lane == s, slot[node, s].astype(f32), info)
    copies = []
    for q in range(4):
        for h in range(2):
            for e in range(4):
                p = place[node, 16 * h + 4 * q + e]
                for ul in range(2):
                    at = pl.multiple_of((ul * 4 + (p & 3)) * 32, 32)
                    v = got[p >> 2, pl.ds(at, 32), :]
                    v = jnp.where(p < lens[ul], v, 0.0)
                    row = ((h * 4 + e) * 2 + ul) * 32
                    buf[q, row : row + 32, :] = v
        buf[q, 512:520, :] = info
        copies.append(pltpu.make_async_copy(buf.at[q], out.at[q], sems.at[q]))
        copies[-1].start()
    for i, v in enumerate((v0, v1, v2, v3)):
        copies.append(pltpu.make_async_copy(buf.at[(y + i) & 3, :512], v, sems.at[4 + i]))
        copies[-1].start()
    for c in copies:
        c.wait()


def fill(pos, lhi, llo, node, src, row, ys):
    xl, core = pos[2], pos[4]
    for p in range(4):
        half = xl if p < 2 else 1 - xl
        pair = core if p % 2 == 0 else 1 - core
        for b in range(2):
            e = half * 4 + pair * 2 + b
            for ul in range(2):
                r = pl.multiple_of((e * 2 + ul) * 32, 32)
                hi, lo = split(src[row, pl.ds(r, 32), :])
                at = pl.multiple_of((p * 2 + b) * B + ys * 32, 32)
                lhi[node, pl.ds(at, 32), ul * B : (ul + 1) * B] = hi
                llo[node, pl.ds(at, 32), ul * B : (ul + 1) * B] = lo


def fill_kernel(pos, l0, lu, ld, lhi, llo):
    y = pos[1]

    def step(node, _):
        fill(pos, lhi, llo, node, l0, node, y)
        fill(pos, lhi, llo, node, lu, node, (y + 3) & 3)
        fill(pos, lhi, llo, node, ld, node, (y + 1) & 3)
        return 0

    lax.fori_loop(0, 4, step, 0)


def product_kernel(first, *refs):
    if first:
        (pos, slots, lhi_in, llo_in, lf1, lf2, own, own_c, side, side_c,
         o0, o1, o2, o3, lhi, llo, selhi, sello) = refs
        outs = ((2, o2), (1, o1), (3, o3), (0, o0))
        pieces = ((own,), (own_c,), (side,), (side_c,))
    else:
        (pos, slots, lhi, llo, top, bot, top_c, bot_c, side, side_c,
         o0, o1, o2, o3, selhi, sello) = refs
        outs = ((2, o2), (1, o1), (3, o3), (0, o0))
        pieces = ((top, bot), (top_c, bot_c), (side,), (side_c,))
    h, y, xl, z, core = pos[0], pos[1], pos[2], pos[3], pos[4]
    at_half = (xl, xl, 1 - xl, 1 - xl)
    at_pair = (core, 1 - core, core, 1 - core)

    if first:

        def fill_far(i, _):
            fill(pos, lhi, llo, i, lf1, i, (y + 2) & 3)
            fill(pos, lhi, llo, i + 2, lf2, i, (y + 2) & 3)
            return 0

        lax.fori_loop(0, 2, fill_far, 0)

    m0 = 16 * (h if first else 1 - h) + 4 * y
    for k, (i, dst) in enumerate(outs):
        node = (z + i) & 3
        for m in range(4):
            cm = slots[node, m0 + m] & 7
            for p in range(4):
                for b in range(2):
                    ck = slots[node, 16 * at_half[p] + 4 * z + 2 * at_pair[p] + b] & 3
                    lanes = pl.ds(pl.multiple_of(ck * B, B), B)
                    if len(pieces[p]) == 1:
                        blk = pieces[p][0][pl.ds(pl.multiple_of(cm * B, B), B), lanes]
                    else:
                        sub = pl.ds(pl.multiple_of((cm & 3) * B, B), B)
                        blk = jnp.where(cm < 4, pieces[p][0][sub, lanes], pieces[p][1][sub, lanes])
                    hi, lo = split(blk)
                    e = p * 2 + b
                    selhi[k & 1, m * B : (m + 1) * B, e * B : (e + 1) * B] = hi
                    sello[k & 1, m * B : (m + 1) * B, e * B : (e + 1) * B] = lo
        bh = lhi[node]
        bl = llo[node]
        ah = selhi[k & 1]
        dst[...] = dot(ah, bh) + (dot(ah, bl) + dot(sello[k & 1], bh))


def product(first, *args):
    out = [shape(512, 256)] * 4
    if first:
        out = out + [jax.ShapeDtypeStruct((4, 1024, 256), bf16)] * 2
    return call(
        lambda *refs: product_kernel(first, *refs),
        out,
        [smem] * 2 + [vmem] * (len(args) - 2),
        [vmem] * len(out),
        [pltpu.VMEM((2, 512, 1024), bf16), pltpu.VMEM((2, 512, 1024), bf16)],
        mib=14,
        name="product_own" if first else "product_far",
        alias={2: 4, 3: 5} if first else {},
    )(*args)


def half_rows(h, y, rows, buf):
    for e in range(4):
        for i, src in enumerate(rows):
            to = pl.multiple_of(e * B + ((y - i) & 3) * 32, 32)
            for ul in range(2):
                at = pl.multiple_of(((h * 4 + e) * 2 + ul) * 32, 32)
                buf[pl.ds(to, 32), ul * B : (ul + 1) * B] = src[pl.ds(at, 32), :]
    return buf[...]


def far_kernel(o0, q1, q2, up, low):
    t = -(o0[...] + (q1[...] + q2[...])).T
    up[...] = t[:B]
    low[...] = t[B:]


def prods_kernel(pos, n0, q1, q2, up, low, v0, v1, v2, v3, near, prods, buf):
    h, y = pos[0], pos[1]
    rows = (v0, v1, v2, v3)
    t = -(n0[...] + (q1[...] + q2[...])).T
    near[...] = t
    s = dot3(t, half_rows(h, y, rows, buf))
    s = s + dot3(jnp.concatenate([up[...], low[...]], axis=0), half_rows(1 - h, y, rows, buf))
    prods[0] = s[:B, :B]
    prods[1] = s[:B, B:]
    prods[2] = s[B:, B:]


def rows_kernel(pos, place, slot, ulen, llen, mine, other_up, other_low, parent, up, low):
    h, y = pos[0], pos[1]
    r = h * 4 + y
    up[...] = jnp.zeros_like(up)
    low[...] = jnp.zeros_like(low)
    for k, src_up, src_low in ((0, mine.at[:B], mine.at[B:]), (1, other_up, other_low)):
        node = h if k == 0 else 1 - h
        lp = parent[node].T
        for e in range(4):
            p = place[node, 4 * r + e]
            at = pl.multiple_of((slot[node, 4 * r + e] & 7) * B, B)
            gu = jnp.where(p < ulen[node], src_up[:, e * B : (e + 1) * B], 0.0)
            gl = src_low[:, e * B : (e + 1) * B] - dot3(lp, gu)
            gl = jnp.where(p < llen[node], gl, 0.0)
            up[node, :, pl.ds(at, B)] = gu
            low[node, :, pl.ds(at, B)] = gl


def diag_kernel(pos, mine, other, uinv, linv, parent, du, pr, dl):
    h = pos[0]
    for k, src in ((0, mine), (1, other)):
        node = h if k == 0 else 1 - h
        lp = parent[node]
        lpt = lp.T
        cross = src[1]
        d = uinv[node] - src[0].T
        row = -(dot3(d, lp) + cross)
        low = src[2].T - dot3(cross.T, lp)
        du[node] = d
        pr[node] = row
        dl[node] = linv[node] - dot3(lpt, row) - low


def call(kernel, out_shape, in_specs, out_specs, scratch=(), mib=16, name=None, alias={}):
    return pl.pallas_call(
        kernel,
        out_shape=out_shape,
        in_specs=in_specs,
        out_specs=out_specs,
        scratch_shapes=list(scratch),
        compiler_params=params(mib),
        name=name,
        input_output_aliases=alias,
    )


def shape(*s):
    return jax.ShapeDtypeStruct(s, f32)


def body(
    ainv_top,
    block_owner,
    upper_list,
    upper_len,
    upper_panel,
    upper_dinv,
    lower_len,
    lower_panel,
    lower_parent,
    lower_dinv,
):
    pos = jnp.stack([lax.axis_index(n) for n in ("xh", "y", "xl", "z", "core")]).astype(jnp.int32)
    pp = lax.ppermute
    mirror = [(0, 3), (1, 2), (2, 1), (3, 0)]
    ints = jax.ShapeDtypeStruct((2, 32), jnp.int32)
    place, slot = call(
        sort_kernel, [ints] * 2, [smem] * 2, [smem] * 2, [pltpu.SMEM((64,), jnp.int32)], name="sort"
    )(block_owner, upper_list)
    sliced = call(
        slice_kernel, pltpu.HBM((8, 2, 4, 32, B), f32), [hbm] * 2, hbm, [pltpu.SemaphoreType.DMA], name="slices"
    )(
        pltpu.with_memory_space_constraint(upper_panel.reshape(2, 4, B, B), pltpu.HBM),
        pltpu.with_memory_space_constraint(lower_panel.reshape(2, 4, B, B), pltpu.HBM),
    )
    got = swap_all(sliced.reshape(8, 256, B), ROW)
    a = ainv_top
    a_nr = pp(a, "xl", shift(2, 1))
    a_fr = pp(a, RING, mirror)
    a_co = pp(a, "core", shift(2, 1))
    a_nr, a_fr = lax.optimization_barrier((a_nr, a_fr))
    got, a_co = lax.optimization_barrier((got, a_co))
    ordered, v0, v1, v2, v3 = call(
        order_kernel,
        [pltpu.HBM((4, 520, B), f32)] + [pltpu.HBM((512, B), f32)] * 4,
        [smem] * 5 + [vmem],
        [hbm] * 5,
        [pltpu.VMEM((4, 520, B), f32), pltpu.SemaphoreType.DMA((8,))],
        name="order",
    )(pos, place, slot, upper_len, lower_len, got)
    l0 = swap_all(ordered, "z")
    v1, v2, v3 = (pp(v, "y", shift(4, i + 1)) for i, v in enumerate((v1, v2, v3)))
    l0, v1, v2, v3 = lax.optimization_barrier((l0, v1, v2, v3))
    lu = pp(l0, "y", shift(4, 1))
    ld = pp(l0, "y", shift(4, 3))
    a_f1 = pp(a_nr[:512], RING, mirror)
    a_f2 = pp(a_fr[512:], "xl", shift(2, 1))
    c_nr = pp(a_nr, "core", shift(2, 1))
    lf1 = pp(lu[:2], "y", shift(4, 1))
    lf2 = pp(ld[2:], "y", shift(4, 3))
    k_fr, lf1, lf2 = lax.optimization_barrier((a_fr, lf1, lf2))
    c_fr = pp(k_fr, "core", shift(2, 1))
    parts = jax.ShapeDtypeStruct((4, 1024, 256), bf16)
    hi, lo = call(fill_kernel, [parts] * 2, [smem] + [vmem] * 3, [vmem] * 2, mib=14, name="fill")(pos, l0, lu, ld)
    slots = l0[:, 512, :32].astype(jnp.int32)
    n0, n1, n2, n3, hi, lo = product(True, pos, slots, hi, lo, lf1, lf2, a, a_co, a_nr, c_nr)
    a_f1, a_f2, n0 = lax.optimization_barrier((a_f1, a_f2, n0))
    c_f1 = pp(a_f1, "core", shift(2, 1))
    c_f2 = pp(a_f2, "core", shift(2, 1))
    ra = pp(n2, "z", shift(4, 1))
    q3 = pp(n3, "z", shift(4, 3))
    o0, o1, o2, o3 = product(False, pos, slots, hi, lo, a_f1, a_f2, c_f1, c_f2, a_fr, c_fr)
    o1, ra = lax.optimization_barrier((o1, ra))
    o2, q3 = lax.optimization_barrier((o2, q3))
    q1 = pp(o1, "z", shift(4, 1))
    rb = pp(o2, "z", shift(4, 3))
    near_up = pp(n1 + ra, "z", shift(4, 1))
    far_dn = pp(o3 + rb, "z", shift(4, 3))
    far_up, far_low = call(far_kernel, [shape(B, 512)] * 2, [vmem] * 3, [vmem] * 2, mib=8, name="far")(o0, q1, far_dn)
    mine, prods = call(
        prods_kernel,
        [shape(256, 512), shape(3, B, B)],
        [smem] + [vmem] * 9,
        [vmem] * 2,
        [pltpu.VMEM((512, 256), f32)],
        mib=16,
        name="prods",
    )(pos, n0, near_up, q3, far_up, far_low, v0, v1, v2, v3)
    s1 = pp(prods, "y", shift(4, 1))
    s2 = pp(prods, "y", shift(4, 2))
    s3 = pp(prods, "y", shift(4, 3))
    other_up = pp(far_up, "xh", shift(2, 1))
    far_low, other_up = lax.optimization_barrier((far_low, other_up))
    other_low = pp(far_low, "xh", shift(2, 1))
    mine_sum = (prods + s1) + (s2 + s3)
    other_sum = pp(mine_sum, "xh", shift(2, 1))
    upper_rows, lower_rows = call(
        rows_kernel, [shape(2, B, 1024)] * 2, [smem] * 5 + [vmem] * 4, [vmem] * 2, name="rows"
    )(pos, place, slot, upper_len, lower_len, mine, other_up, other_low, lower_parent)
    other_sum, upper_rows = lax.optimization_barrier((other_sum, upper_rows))
    diag_up, parent_row, diag_low = call(
        diag_kernel, [shape(2, B, B)] * 3, [smem] + [vmem] * 5, [vmem] * 3, name="diag"
    )(pos, mine_sum, other_sum, upper_dinv, lower_dinv, lower_parent)
    return (upper_rows, diag_up, lower_rows, parent_row, diag_low)


def solution(mesh):
    fine = Mesh(mesh.devices.reshape(2, 4, 2, 4, 2), ("xh", "y", "xl", "z", "core"))
    row = ("xh", "y")
    col = ("xl", "z", "core")
    in_specs = (
        P(row, col),
        P(),
        P(col, None),
        P(col),
        P(col, row, None),
        P(col, None, None),
        P(col),
        P(col, row, None),
        P(col, None, None),
        P(col, None, None),
    )
    out_specs = (
        P(col, None, row),
        P(col, None, None),
        P(col, None, row),
        P(col, None, None),
        P(col, None, None),
    )
    return jax.shard_map(body, mesh=fine, in_specs=in_specs, out_specs=out_specs, check_vma=False)
```

```python
import jax
import jax.numpy as jnp
from jax import lax
from jax.experimental import pallas as pl
from jax.experimental.pallas import tpu as pltpu
from jax.sharding import Mesh, PartitionSpec as P

B = 128
MIB = 1 << 20
ROW = ("xh", "y")
RING = ("xh", "xl")
f32 = jnp.float32
bf16 = jnp.bfloat16

smem = pl.BlockSpec(memory_space=pltpu.SMEM)
vmem = pl.BlockSpec(memory_space=pltpu.VMEM)
hbm = pl.BlockSpec(memory_space=pltpu.HBM)


def params(mib):
    return pltpu.CompilerParams(vmem_limit_bytes=mib * MIB)


def shift(n, s):
    return [(i, (i + s) % n) for i in range(n)]


def swap_all(x, axis):
    return lax.all_to_all(x, axis, split_axis=0, concat_axis=0, tiled=True)


def split(x):
    hi = x.astype(bf16)
    return hi, (x - hi.astype(f32)).astype(bf16)


def dot(a, b):
    return jnp.dot(a, b, preferred_element_type=f32)


def dot3(a, b):
    ah, al = split(a)
    bh, bl = split(b)
    return dot(ah, bh) + (dot(ah, bl) + dot(al, bh))


def sort_kernel(owner, names, place, slot, inv):
    for node in range(2):

        def clear(t, _):
            inv[t] = -1
            return 0

        def mark(q, _):
            inv[owner[names[node, q]]] = q
            return 0

        def pick(g, _):
            t = 4 * g
            lo = jnp.where(inv[t] >= 0, 0, jnp.where(inv[t + 1] >= 0, 1, 2))
            hi = jnp.where(inv[t + 3] >= 0, 3, jnp.where(inv[t + 2] >= 0, 2, 1))
            place[node, 2 * g] = inv[t + lo]
            slot[node, 2 * g] = t + lo
            place[node, 2 * g + 1] = inv[t + hi]
            slot[node, 2 * g + 1] = t + hi
            return 0

        lax.fori_loop(0, 64, clear, 0)
        lax.fori_loop(0, 32, mark, 0)
        lax.fori_loop(0, 16, pick, 0)


def slice_kernel(up, low, out, buf, sems):
    copies = []
    for node in range(2):
        for q in range(4):
            for ul, src in enumerate((up, low)):
                copies.append(
                    pltpu.make_async_copy(
                        src.at[node, :, q * 32 : (q + 1) * 32, :], buf.at[node * 4 + q, ul], sems.at[len(copies)]
                    )
                )
    for c in copies:
        c.start()
    for c in copies:
        c.wait()
    whole = pltpu.make_async_copy(buf, out, sems.at[len(copies)])
    whole.start()
    whole.wait()


def order_kernel(pos, place, slot, ulen, llen, got, out, v0, v1, v2, v3, buf, sems):
    node, y = pos[0], pos[1]
    lens = (ulen[node], llen[node])
    lane = lax.broadcasted_iota(jnp.int32, (8, B), 1)
    info = jnp.zeros((8, B), f32)
    for s in range(32):
        info = jnp.where(lane == s, slot[node, s].astype(f32), info)
    copies = []
    for q in range(4):
        for h in range(2):
            for e in range(4):
                p = place[node, 16 * h + 4 * q + e]
                for ul in range(2):
                    at = pl.multiple_of((ul * 4 + (p & 3)) * 32, 32)
                    v = got[p >> 2, pl.ds(at, 32), :]
                    v = jnp.where(p < lens[ul], v, 0.0)
                    row = ((h * 4 + e) * 2 + ul) * 32
                    buf[q, row : row + 32, :] = v
        buf[q, 512:520, :] = info
        copies.append(pltpu.make_async_copy(buf.at[q], out.at[q], sems.at[q]))
        copies[-1].start()
    for i, v in enumerate((v0, v1, v2, v3)):
        copies.append(pltpu.make_async_copy(buf.at[(y + i) & 3, :512], v, sems.at[4 + i]))
        copies[-1].start()
    for c in copies:
        c.wait()


def fill(pos, lhi, llo, node, src, row, ys):
    xl, core = pos[2], pos[4]
    for p in range(4):
        half = xl if p < 2 else 1 - xl
        pair = core if p % 2 == 0 else 1 - core
        for b in range(2):
            e = half * 4 + pair * 2 + b
            for ul in range(2):
                r = pl.multiple_of((e * 2 + ul) * 32, 32)
                hi, lo = split(src[row, pl.ds(r, 32), :])
                at = pl.multiple_of((p * 2 + b) * B + ys * 32, 32)
                lhi[node, pl.ds(at, 32), ul * B : (ul + 1) * B] = hi
                llo[node, pl.ds(at, 32), ul * B : (ul + 1) * B] = lo


def fill_kernel(pos, l0, lu, ld, lhi, llo):
    y = pos[1]

    def step(node, _):
        fill(pos, lhi, llo, node, l0, node, y)
        fill(pos, lhi, llo, node, lu, node, (y + 3) & 3)
        fill(pos, lhi, llo, node, ld, node, (y + 1) & 3)
        return 0

    lax.fori_loop(0, 4, step, 0)


def product_kernel(first, *refs):
    if first:
        (pos, slots, lhi_in, llo_in, lf1, lf2, own, own_c, side, side_c,
         o0, o1, o2, o3, lhi, llo, selhi, sello) = refs
        outs = ((2, o2), (1, o1), (3, o3), (0, o0))
        pieces = ((own,), (own_c,), (side,), (side_c,))
    else:
        (pos, slots, lhi, llo, top, bot, top_c, bot_c, side, side_c,
         o0, o1, o2, o3, selhi, sello) = refs
        outs = ((2, o2), (1, o1), (3, o3), (0, o0))
        pieces = ((top, bot), (top_c, bot_c), (side,), (side_c,))
    h, y, xl, z, core = pos[0], pos[1], pos[2], pos[3], pos[4]
    at_half = (xl, xl, 1 - xl, 1 - xl)
    at_pair = (core, 1 - core, core, 1 - core)

    if first:

        def fill_far(i, _):
            fill(pos, lhi, llo, i, lf1, i, (y + 2) & 3)
            fill(pos, lhi, llo, i + 2, lf2, i, (y + 2) & 3)
            return 0

        lax.fori_loop(0, 2, fill_far, 0)

    m0 = 16 * (h if first else 1 - h) + 4 * y
    for k, (i, dst) in enumerate(outs):
        node = (z + i) & 3
        for m in range(4):
            cm = slots[node, m0 + m] & 7
            for p in range(4):
                for b in range(2):
                    ck = slots[node, 16 * at_half[p] + 4 * z + 2 * at_pair[p] + b] & 3
                    lanes = pl.ds(pl.multiple_of(ck * B, B), B)
                    if len(pieces[p]) == 1:
                        blk = pieces[p][0][pl.ds(pl.multiple_of(cm * B, B), B), lanes]
                    else:
                        sub = pl.ds(pl.multiple_of((cm & 3) * B, B), B)
                        blk = jnp.where(cm < 4, pieces[p][0][sub, lanes], pieces[p][1][sub, lanes])
                    hi, lo = split(blk)
                    e = p * 2 + b
                    selhi[k & 1, m * B : (m + 1) * B, e * B : (e + 1) * B] = hi
                    sello[k & 1, m * B : (m + 1) * B, e * B : (e + 1) * B] = lo
        bh = lhi[node]
        bl = llo[node]
        ah = selhi[k & 1]
        dst[...] = dot(ah, bh) + (dot(ah, bl) + dot(sello[k & 1], bh))


def product(first, *args):
    out = [shape(512, 256)] * 4
    if first:
        out = out + [jax.ShapeDtypeStruct((4, 1024, 256), bf16)] * 2
    return call(
        lambda *refs: product_kernel(first, *refs),
        out,
        [smem] * 2 + [vmem] * (len(args) - 2),
        [vmem] * len(out),
        [pltpu.VMEM((2, 512, 1024), bf16), pltpu.VMEM((2, 512, 1024), bf16)],
        mib=14,
        name="product_own" if first else "product_far",
        alias={2: 4, 3: 5} if first else {},
    )(*args)


def half_rows(h, y, rows, buf):
    for e in range(4):
        for i, src in enumerate(rows):
            to = pl.multiple_of(e * B + ((y - i) & 3) * 32, 32)
            for ul in range(2):
                at = pl.multiple_of(((h * 4 + e) * 2 + ul) * 32, 32)
                buf[pl.ds(to, 32), ul * B : (ul + 1) * B] = src[pl.ds(at, 32), :]
    return buf[...]


def far_kernel(o0, q1, q2, up, low):
    t = -(o0[...] + (q1[...] + q2[...])).T
    up[...] = t[:B]
    low[...] = t[B:]


def prods_kernel(pos, n0, q1, q2, up, low, v0, v1, v2, v3, near, prods, buf):
    h, y = pos[0], pos[1]
    rows = (v0, v1, v2, v3)
    t = -(n0[...] + (q1[...] + q2[...])).T
    near[...] = t
    s = dot3(t, half_rows(h, y, rows, buf))
    s = s + dot3(jnp.concatenate([up[...], low[...]], axis=0), half_rows(1 - h, y, rows, buf))
    prods[0] = s[:B, :B]
    prods[1] = s[:B, B:]
    prods[2] = s[B:, B:]


def rows_kernel(pos, place, slot, ulen, llen, mine, other_up, other_low, parent, up, low):
    h, y = pos[0], pos[1]
    r = h * 4 + y
    up[...] = jnp.zeros_like(up)
    low[...] = jnp.zeros_like(low)
    for k, src_up, src_low in ((0, mine.at[:B], mine.at[B:]), (1, other_up, other_low)):
        node = h if k == 0 else 1 - h
        lp = parent[node].T
        for e in range(4):
            p = place[node, 4 * r + e]
            at = pl.multiple_of((slot[node, 4 * r + e] & 7) * B, B)
            gu = jnp.where(p < ulen[node], src_up[:, e * B : (e + 1) * B], 0.0)
            gl = src_low[:, e * B : (e + 1) * B] - dot3(lp, gu)
            gl = jnp.where(p < llen[node], gl, 0.0)
            up[node, :, pl.ds(at, B)] = gu
            low[node, :, pl.ds(at, B)] = gl


def diag_kernel(pos, mine, other, uinv, linv, parent, du, pr, dl):
    h = pos[0]
    for k, src in ((0, mine), (1, other)):
        node = h if k == 0 else 1 - h
        lp = parent[node]
        lpt = lp.T
        cross = src[1]
        d = uinv[node] - src[0].T
        row = -(dot3(d, lp) + cross)
        low = src[2].T - dot3(cross.T, lp)
        du[node] = d
        pr[node] = row
        dl[node] = linv[node] - dot3(lpt, row) - low


def call(kernel, out_shape, in_specs, out_specs, scratch=(), mib=16, name=None, alias={}):
    return pl.pallas_call(
        kernel,
        out_shape=out_shape,
        in_specs=in_specs,
        out_specs=out_specs,
        scratch_shapes=list(scratch),
        compiler_params=params(mib),
        name=name,
        input_output_aliases=alias,
    )


def shape(*s):
    return jax.ShapeDtypeStruct(s, f32)


def body(
    ainv_top,
    block_owner,
    upper_list,
    upper_len,
    upper_panel,
    upper_dinv,
    lower_len,
    lower_panel,
    lower_parent,
    lower_dinv,
):
    pos = jnp.stack([lax.axis_index(n) for n in ("xh", "y", "xl", "z", "core")]).astype(jnp.int32)
    pp = lax.ppermute
    mirror = [(0, 3), (1, 2), (2, 1), (3, 0)]
    ints = jax.ShapeDtypeStruct((2, 32), jnp.int32)
    place, slot = call(
        sort_kernel, [ints] * 2, [smem] * 2, [smem] * 2, [pltpu.SMEM((64,), jnp.int32)], name="sort"
    )(block_owner, upper_list)
    sliced = call(
        slice_kernel, pltpu.HBM((8, 2, 4, 32, B), f32), [hbm] * 2, hbm, [pltpu.VMEM((8, 2, 4, 32, B), f32), pltpu.SemaphoreType.DMA((17,))], name="slices"
    )(
        pltpu.with_memory_space_constraint(upper_panel.reshape(2, 4, B, B), pltpu.HBM),
        pltpu.with_memory_space_constraint(lower_panel.reshape(2, 4, B, B), pltpu.HBM),
    )
    got = swap_all(sliced.reshape(8, 256, B), ROW)
    a = ainv_top
    a_nr = pp(a, "xl", shift(2, 1))
    a_fr = pp(a, RING, mirror)
    a_co = pp(a, "core", shift(2, 1))
    a_nr, a_fr = lax.optimization_barrier((a_nr, a_fr))
    got, a_co = lax.optimization_barrier((got, a_co))
    ordered, v0, v1, v2, v3 = call(
        order_kernel,
        [pltpu.HBM((4, 520, B), f32)] + [pltpu.HBM((512, B), f32)] * 4,
        [smem] * 5 + [vmem],
        [hbm] * 5,
        [pltpu.VMEM((4, 520, B), f32), pltpu.SemaphoreType.DMA((8,))],
        name="order",
    )(pos, place, slot, upper_len, lower_len, got)
    l0 = swap_all(ordered, "z")
    v1, v2, v3 = (pp(v, "y", shift(4, i + 1)) for i, v in enumerate((v1, v2, v3)))
    l0, v1, v2, v3 = lax.optimization_barrier((l0, v1, v2, v3))
    lu = pp(l0, "y", shift(4, 1))
    ld = pp(l0, "y", shift(4, 3))
    a_f1 = pp(a_nr[:512], RING, mirror)
    a_f2 = pp(a_fr[512:], "xl", shift(2, 1))
    c_nr = pp(a_nr, "core", shift(2, 1))
    lf1 = pp(lu[:2], "y", shift(4, 1))
    lf2 = pp(ld[2:], "y", shift(4, 3))
    k_fr, lf1, lf2 = lax.optimization_barrier((a_fr, lf1, lf2))
    c_fr = pp(k_fr, "core", shift(2, 1))
    parts = jax.ShapeDtypeStruct((4, 1024, 256), bf16)
    hi, lo = call(fill_kernel, [parts] * 2, [smem] + [vmem] * 3, [vmem] * 2, mib=14, name="fill")(pos, l0, lu, ld)
    slots = l0[:, 512, :32].astype(jnp.int32)
    n0, n1, n2, n3, hi, lo = product(True, pos, slots, hi, lo, lf1, lf2, a, a_co, a_nr, c_nr)
    a_f1, a_f2, n0 = lax.optimization_barrier((a_f1, a_f2, n0))
    c_f1 = pp(a_f1, "core", shift(2, 1))
    c_f2 = pp(a_f2, "core", shift(2, 1))
    ra = pp(n2, "z", shift(4, 1))
    q3 = pp(n3, "z", shift(4, 3))
    o0, o1, o2, o3 = product(False, pos, slots, hi, lo, a_f1, a_f2, c_f1, c_f2, a_fr, c_fr)
    o1, ra = lax.optimization_barrier((o1, ra))
    o2, q3 = lax.optimization_barrier((o2, q3))
    q1 = pp(o1, "z", shift(4, 1))
    rb = pp(o2, "z", shift(4, 3))
    near_up = pp(n1 + ra, "z", shift(4, 1))
    far_dn = pp(o3 + rb, "z", shift(4, 3))
    far_up, far_low = call(far_kernel, [shape(B, 512)] * 2, [vmem] * 3, [vmem] * 2, mib=8, name="far")(o0, q1, far_dn)
    mine, prods = call(
        prods_kernel,
        [shape(256, 512), shape(3, B, B)],
        [smem] + [vmem] * 9,
        [vmem] * 2,
        [pltpu.VMEM((512, 256), f32)],
        mib=16,
        name="prods",
    )(pos, n0, near_up, q3, far_up, far_low, v0, v1, v2, v3)
    s1 = pp(prods, "y", shift(4, 1))
    s2 = pp(prods, "y", shift(4, 2))
    s3 = pp(prods, "y", shift(4, 3))
    other_up = pp(far_up, "xh", shift(2, 1))
    far_low, other_up = lax.optimization_barrier((far_low, other_up))
    other_low = pp(far_low, "xh", shift(2, 1))
    mine_sum = (prods + s1) + (s2 + s3)
    other_sum = pp(mine_sum, "xh", shift(2, 1))
    upper_rows, lower_rows = call(
        rows_kernel, [shape(2, B, 1024)] * 2, [smem] * 5 + [vmem] * 4, [vmem] * 2, name="rows"
    )(pos, place, slot, upper_len, lower_len, mine, other_up, other_low, lower_parent)
    other_sum, upper_rows = lax.optimization_barrier((other_sum, upper_rows))
    diag_up, parent_row, diag_low = call(
        diag_kernel, [shape(2, B, B)] * 3, [smem] + [vmem] * 5, [vmem] * 3, name="diag"
    )(pos, mine_sum, other_sum, upper_dinv, lower_dinv, lower_parent)
    return (upper_rows, diag_up, lower_rows, parent_row, diag_low)


def solution(mesh):
    fine = Mesh(mesh.devices.reshape(2, 4, 2, 4, 2), ("xh", "y", "xl", "z", "core"))
    row = ("xh", "y")
    col = ("xl", "z", "core")
    in_specs = (
        P(row, col),
        P(),
        P(col, None),
        P(col),
        P(col, row, None),
        P(col, None, None),
        P(col),
        P(col, row, None),
        P(col, None, None),
        P(col, None, None),
    )
    out_specs = (
        P(col, None, row),
        P(col, None, None),
        P(col, None, row),
        P(col, None, None),
        P(col, None, None),
    )
    return jax.shard_map(body, mesh=fine, in_specs=in_specs, out_specs=out_specs, check_vma=False)
```

```python
import jax
import jax.numpy as jnp
from jax import lax
from jax.experimental import pallas as pl
from jax.experimental.pallas import tpu as pltpu
from jax.sharding import Mesh, PartitionSpec as P

B = 128
MIB = 1 << 20
ROW = ("xh", "y")
RING = ("xh", "xl")
f32 = jnp.float32
bf16 = jnp.bfloat16

smem = pl.BlockSpec(memory_space=pltpu.SMEM)
vmem = pl.BlockSpec(memory_space=pltpu.VMEM)
hbm = pl.BlockSpec(memory_space=pltpu.HBM)


def params(mib):
    return pltpu.CompilerParams(vmem_limit_bytes=mib * MIB)


def shift(n, s):
    return [(i, (i + s) % n) for i in range(n)]


def swap_all(x, axis):
    return lax.all_to_all(x, axis, split_axis=0, concat_axis=0, tiled=True)


def split(x):
    hi = x.astype(bf16)
    return hi, (x - hi.astype(f32)).astype(bf16)


def dot(a, b):
    return jnp.dot(a, b, preferred_element_type=f32)


def dot3(a, b):
    ah, al = split(a)
    bh, bl = split(b)
    return dot(ah, bh) + (dot(ah, bl) + dot(al, bh))


def sort_kernel(owner, names, place, slot, inv):
    for node in range(2):

        def clear(t, _):
            inv[t] = -1
            return 0

        def mark(q, _):
            inv[owner[names[node, q]]] = q
            return 0

        def pick(g, _):
            t = 4 * g
            lo = jnp.where(inv[t] >= 0, 0, jnp.where(inv[t + 1] >= 0, 1, 2))
            hi = jnp.where(inv[t + 3] >= 0, 3, jnp.where(inv[t + 2] >= 0, 2, 1))
            place[node, 2 * g] = inv[t + lo]
            slot[node, 2 * g] = t + lo
            place[node, 2 * g + 1] = inv[t + hi]
            slot[node, 2 * g + 1] = t + hi
            return 0

        lax.fori_loop(0, 64, clear, 0)
        lax.fori_loop(0, 32, mark, 0)
        lax.fori_loop(0, 16, pick, 0)


def slice_kernel(up, low, out, buf, sems):
    copies = []
    for node in range(2):
        for q in range(4):
            for ul, src in enumerate((up, low)):
                copies.append(
                    pltpu.make_async_copy(
                        src.at[node, :, q * 32 : (q + 1) * 32, :], buf.at[node * 4 + q, ul], sems.at[len(copies)]
                    )
                )
    for c in copies:
        c.start()
    for c in copies:
        c.wait()
    whole = pltpu.make_async_copy(buf, out, sems.at[len(copies)])
    whole.start()
    whole.wait()


def order_kernel(pos, place, slot, ulen, llen, got, out, v0, v1, v2, v3, buf, sems):
    node, y = pos[0], pos[1]
    lens = (ulen[node], llen[node])
    lane = lax.broadcasted_iota(jnp.int32, (8, B), 1)
    info = jnp.zeros((8, B), f32)
    for s in range(32):
        info = jnp.where(lane == s, slot[node, s].astype(f32), info)
    copies = []
    for q in range(4):
        for h in range(2):
            for e in range(4):
                p = place[node, 16 * h + 4 * q + e]
                for ul in range(2):
                    at = pl.multiple_of((ul * 4 + (p & 3)) * 32, 32)
                    v = got[p >> 2, pl.ds(at, 32), :]
                    v = jnp.where(p < lens[ul], v, 0.0)
                    row = ((h * 4 + e) * 2 + ul) * 32
                    buf[q, row : row + 32, :] = v
        buf[q, 512:520, :] = info
        copies.append(pltpu.make_async_copy(buf.at[q], out.at[q], sems.at[q]))
        copies[-1].start()
    for i, v in enumerate((v0, v1, v2, v3)):
        copies.append(pltpu.make_async_copy(buf.at[(y + i) & 3, :512], v, sems.at[4 + i]))
        copies[-1].start()
    for c in copies:
        c.wait()


def fill(pos, lhi, llo, node, src, row, ys):
    xl, core = pos[2], pos[4]
    for p in range(4):
        half = xl if p < 2 else 1 - xl
        pair = core if p % 2 == 0 else 1 - core
        for b in range(2):
            e = half * 4 + pair * 2 + b
            for ul in range(2):
                r = pl.multiple_of((e * 2 + ul) * 32, 32)
                hi, lo = split(src[row, pl.ds(r, 32), :])
                at = pl.multiple_of((p * 2 + b) * B + ys * 32, 32)
                lhi[node, pl.ds(at, 32), ul * B : (ul + 1) * B] = hi
                llo[node, pl.ds(at, 32), ul * B : (ul + 1) * B] = lo


def fill_kernel(pos, l0, lu, ld, lhi, llo):
    y = pos[1]

    def step(node, _):
        fill(pos, lhi, llo, node, l0, node, y)
        fill(pos, lhi, llo, node, lu, node, (y + 3) & 3)
        fill(pos, lhi, llo, node, ld, node, (y + 1) & 3)
        return 0

    lax.fori_loop(0, 4, step, 0)


def product_kernel(first, *refs):
    if first:
        (pos, slots, lhi_in, llo_in, lf1, lf2, own, own_c, side, side_c,
         o0, o1, o2, o3, lhi, llo, *sel) = refs
        outs = ((2, o2), (1, o1), (3, o3), (0, o0))
        pieces = ((own,), (own_c,), (side,), (side_c,))
    else:
        (pos, slots, lhi, llo, top, bot, top_c, bot_c, side, side_c,
         o0, o1, o2, o3, *sel) = refs
        outs = ((2, o2), (1, o1), (3, o3), (0, o0))
        pieces = ((top, bot), (top_c, bot_c), (side,), (side_c,))
    h, y, xl, z, core = pos[0], pos[1], pos[2], pos[3], pos[4]
    at_half = (xl, xl, 1 - xl, 1 - xl)
    at_pair = (core, 1 - core, core, 1 - core)

    if first:

        def fill_far(i, _):
            fill(pos, lhi, llo, i, lf1, i, (y + 2) & 3)
            fill(pos, lhi, llo, i + 2, lf2, i, (y + 2) & 3)
            return 0

        lax.fori_loop(0, 2, fill_far, 0)

    m0 = 16 * (h if first else 1 - h) + 4 * y

    def select(k):
        node = (z + outs[k][0]) & 3
        selhi, sello = sel[2 * (k & 1)], sel[2 * (k & 1) + 1]
        for m in range(4):
            cm = slots[node, m0 + m] & 7
            for p in range(4):
                for b in range(2):
                    ck = slots[node, 16 * at_half[p] + 4 * z + 2 * at_pair[p] + b] & 3
                    lanes = pl.ds(pl.multiple_of(ck * B, B), B)
                    if len(pieces[p]) == 1:
                        blk = pieces[p][0][pl.ds(pl.multiple_of(cm * B, B), B), lanes]
                    else:
                        sub = pl.ds(pl.multiple_of((cm & 3) * B, B), B)
                        blk = jnp.where(cm < 4, pieces[p][0][sub, lanes], pieces[p][1][sub, lanes])
                    hi, lo = split(blk)
                    e = p * 2 + b
                    selhi[m * B : (m + 1) * B, e * B : (e + 1) * B] = hi
                    sello[m * B : (m + 1) * B, e * B : (e + 1) * B] = lo

    select(0)
    for k, (i, dst) in enumerate(outs):
        if k < 3:
            select(k + 1)
        node = (z + i) & 3
        ah, al = sel[2 * (k & 1)][...], sel[2 * (k & 1) + 1][...]
        bh, bl = lhi[node], llo[node]
        dst[...] = dot(ah, bh) + (dot(ah, bl) + dot(al, bh))


def product(first, *args):
    out = [shape(512, 256)] * 4
    if first:
        out = out + [jax.ShapeDtypeStruct((4, 1024, 256), bf16)] * 2
    return call(
        lambda *refs: product_kernel(first, *refs),
        out,
        [smem] * 2 + [vmem] * (len(args) - 2),
        [vmem] * len(out),
        [pltpu.VMEM((512, 1024), bf16)] * 4,
        mib=14,
        name="product_own" if first else "product_far",
        alias={2: 4, 3: 5} if first else {},
    )(*args)


def half_rows(h, y, rows, buf):
    for e in range(4):
        for i, src in enumerate(rows):
            to = pl.multiple_of(e * B + ((y - i) & 3) * 32, 32)
            for ul in range(2):
                at = pl.multiple_of(((h * 4 + e) * 2 + ul) * 32, 32)
                buf[pl.ds(to, 32), ul * B : (ul + 1) * B] = src[pl.ds(at, 32), :]
    return buf[...]


def far_kernel(o0, q1, q2, up, low):
    t = -(o0[...] + (q1[...] + q2[...])).T
    up[...] = t[:B]
    low[...] = t[B:]


def prods_kernel(pos, n0, q1, q2, up, low, v0, v1, v2, v3, near, prods, buf):
    h, y = pos[0], pos[1]
    rows = (v0, v1, v2, v3)
    t = -(n0[...] + (q1[...] + q2[...])).T
    near[...] = t
    s = dot3(t, half_rows(h, y, rows, buf))
    s = s + dot3(jnp.concatenate([up[...], low[...]], axis=0), half_rows(1 - h, y, rows, buf))
    prods[0] = s[:B, :B]
    prods[1] = s[:B, B:]
    prods[2] = s[B:, B:]


def rows_kernel(pos, place, slot, ulen, llen, mine, other_up, other_low, parent, up, low):
    h, y = pos[0], pos[1]
    r = h * 4 + y
    up[...] = jnp.zeros_like(up)
    low[...] = jnp.zeros_like(low)
    for k, src_up, src_low in ((0, mine.at[:B], mine.at[B:]), (1, other_up, other_low)):
        node = h if k == 0 else 1 - h
        lp = parent[node].T
        for e in range(4):
            p = place[node, 4 * r + e]
            at = pl.multiple_of((slot[node, 4 * r + e] & 7) * B, B)
            gu = jnp.where(p < ulen[node], src_up[:, e * B : (e + 1) * B], 0.0)
            gl = src_low[:, e * B : (e + 1) * B] - dot3(lp, gu)
            gl = jnp.where(p < llen[node], gl, 0.0)
            up[node, :, pl.ds(at, B)] = gu
            low[node, :, pl.ds(at, B)] = gl


def diag_kernel(pos, mine, other, uinv, linv, parent, du, pr, dl):
    h = pos[0]
    for k, src in ((0, mine), (1, other)):
        node = h if k == 0 else 1 - h
        lp = parent[node]
        lpt = lp.T
        cross = src[1]
        d = uinv[node] - src[0].T
        row = -(dot3(d, lp) + cross)
        low = src[2].T - dot3(cross.T, lp)
        du[node] = d
        pr[node] = row
        dl[node] = linv[node] - dot3(lpt, row) - low


def call(kernel, out_shape, in_specs, out_specs, scratch=(), mib=16, name=None, alias={}):
    return pl.pallas_call(
        kernel,
        out_shape=out_shape,
        in_specs=in_specs,
        out_specs=out_specs,
        scratch_shapes=list(scratch),
        compiler_params=params(mib),
        name=name,
        input_output_aliases=alias,
    )


def shape(*s):
    return jax.ShapeDtypeStruct(s, f32)


def body(
    ainv_top,
    block_owner,
    upper_list,
    upper_len,
    upper_panel,
    upper_dinv,
    lower_len,
    lower_panel,
    lower_parent,
    lower_dinv,
):
    pos = jnp.stack([lax.axis_index(n) for n in ("xh", "y", "xl", "z", "core")]).astype(jnp.int32)
    pp = lax.ppermute
    mirror = [(0, 3), (1, 2), (2, 1), (3, 0)]
    ints = jax.ShapeDtypeStruct((2, 32), jnp.int32)
    place, slot = call(
        sort_kernel, [ints] * 2, [smem] * 2, [smem] * 2, [pltpu.SMEM((64,), jnp.int32)], name="sort"
    )(block_owner, upper_list)
    sliced = call(
        slice_kernel, pltpu.HBM((8, 2, 4, 32, B), f32), [hbm] * 2, hbm, [pltpu.VMEM((8, 2, 4, 32, B), f32), pltpu.SemaphoreType.DMA((17,))], name="slices"
    )(
        pltpu.with_memory_space_constraint(upper_panel.reshape(2, 4, B, B), pltpu.HBM),
        pltpu.with_memory_space_constraint(lower_panel.reshape(2, 4, B, B), pltpu.HBM),
    )
    got = swap_all(sliced.reshape(8, 256, B), ROW)
    a = ainv_top
    a_nr = pp(a, "xl", shift(2, 1))
    a_fr = pp(a, RING, mirror)
    a_co = pp(a, "core", shift(2, 1))
    a_nr, a_fr = lax.optimization_barrier((a_nr, a_fr))
    got, a_co = lax.optimization_barrier((got, a_co))
    ordered, v0, v1, v2, v3 = call(
        order_kernel,
        [pltpu.HBM((4, 520, B), f32)] + [pltpu.HBM((512, B), f32)] * 4,
        [smem] * 5 + [vmem],
        [hbm] * 5,
        [pltpu.VMEM((4, 520, B), f32), pltpu.SemaphoreType.DMA((8,))],
        name="order",
    )(pos, place, slot, upper_len, lower_len, got)
    l0 = swap_all(ordered, "z")
    v1, v2, v3 = (pp(v, "y", shift(4, i + 1)) for i, v in enumerate((v1, v2, v3)))
    l0, v1, v2, v3 = lax.optimization_barrier((l0, v1, v2, v3))
    lu = pp(l0, "y", shift(4, 1))
    ld = pp(l0, "y", shift(4, 3))
    top, bottom, lu, ld = lax.optimization_barrier((a_nr[:512], a_fr[512:], lu, ld))
    a_f1 = pp(top, RING, mirror)
    a_f2 = pp(bottom, "xl", shift(2, 1))
    c_nr = pp(a_nr, "core", shift(2, 1))
    lf1 = pp(lu[:2], "y", shift(4, 1))
    lf2 = pp(ld[2:], "y", shift(4, 3))
    k_fr, lf1, lf2 = lax.optimization_barrier((a_fr, lf1, lf2))
    c_fr = pp(k_fr, "core", shift(2, 1))
    parts = jax.ShapeDtypeStruct((4, 1024, 256), bf16)
    hi, lo = call(fill_kernel, [parts] * 2, [smem] + [vmem] * 3, [vmem] * 2, mib=14, name="fill")(pos, l0, lu, ld)
    slots = l0[:, 512, :32].astype(jnp.int32)
    n0, n1, n2, n3, hi, lo = product(True, pos, slots, hi, lo, lf1, lf2, a, a_co, a_nr, c_nr)
    a_f1, a_f2, n0 = lax.optimization_barrier((a_f1, a_f2, n0))
    c_f1 = pp(a_f1, "core", shift(2, 1))
    c_f2 = pp(a_f2, "core", shift(2, 1))
    ra = pp(n2, "z", shift(4, 1))
    q3 = pp(n3, "z", shift(4, 3))
    o0, o1, o2, o3 = product(False, pos, slots, hi, lo, a_f1, a_f2, c_f1, c_f2, a_fr, c_fr)
    o1, ra = lax.optimization_barrier((o1, ra))
    o2, q3 = lax.optimization_barrier((o2, q3))
    q1 = pp(o1, "z", shift(4, 1))
    rb = pp(o2, "z", shift(4, 3))
    near_up = pp(n1 + ra, "z", shift(4, 1))
    far_dn = pp(o3 + rb, "z", shift(4, 3))
    far_up, far_low = call(far_kernel, [shape(B, 512)] * 2, [vmem] * 3, [vmem] * 2, mib=8, name="far")(o0, q1, far_dn)
    mine, prods = call(
        prods_kernel,
        [shape(256, 512), shape(3, B, B)],
        [smem] + [vmem] * 9,
        [vmem] * 2,
        [pltpu.VMEM((512, 256), f32)],
        mib=16,
        name="prods",
    )(pos, n0, near_up, q3, far_up, far_low, v0, v1, v2, v3)
    s1 = pp(prods, "y", shift(4, 1))
    s2 = pp(prods, "y", shift(4, 2))
    s3 = pp(prods, "y", shift(4, 3))
    other_up = pp(far_up, "xh", shift(2, 1))
    far_low, other_up = lax.optimization_barrier((far_low, other_up))
    other_low = pp(far_low, "xh", shift(2, 1))
    mine_sum = (prods + s1) + (s2 + s3)
    other_sum = pp(mine_sum, "xh", shift(2, 1))
    upper_rows, lower_rows = call(
        rows_kernel, [shape(2, B, 1024)] * 2, [smem] * 5 + [vmem] * 4, [vmem] * 2, name="rows"
    )(pos, place, slot, upper_len, lower_len, mine, other_up, other_low, lower_parent)
    other_sum, upper_rows = lax.optimization_barrier((other_sum, upper_rows))
    diag_up, parent_row, diag_low = call(
        diag_kernel, [shape(2, B, B)] * 3, [smem] + [vmem] * 5, [vmem] * 3, name="diag"
    )(pos, mine_sum, other_sum, upper_dinv, lower_dinv, lower_parent)
    return (upper_rows, diag_up, lower_rows, parent_row, diag_low)


def solution(mesh):
    fine = Mesh(mesh.devices.reshape(2, 4, 2, 4, 2), ("xh", "y", "xl", "z", "core"))
    row = ("xh", "y")
    col = ("xl", "z", "core")
    in_specs = (
        P(row, col),
        P(),
        P(col, None),
        P(col),
        P(col, row, None),
        P(col, None, None),
        P(col),
        P(col, row, None),
        P(col, None, None),
        P(col, None, None),
    )
    out_specs = (
        P(col, None, row),
        P(col, None, None),
        P(col, None, row),
        P(col, None, None),
        P(col, None, None),
    )
    return jax.shard_map(body, mesh=fine, in_specs=in_specs, out_specs=out_specs, check_vma=False)
```

```python
import jax
import jax.numpy as jnp
from jax import lax
from jax.experimental import pallas as pl
from jax.experimental.pallas import tpu as pltpu
from jax.sharding import Mesh, PartitionSpec as P

B = 128
MIB = 1 << 20
ROW = ("xh", "y")
RING = ("xh", "xl")
f32 = jnp.float32
bf16 = jnp.bfloat16

smem = pl.BlockSpec(memory_space=pltpu.SMEM)
vmem = pl.BlockSpec(memory_space=pltpu.VMEM)
hbm = pl.BlockSpec(memory_space=pltpu.HBM)


def params(mib):
    return pltpu.CompilerParams(vmem_limit_bytes=mib * MIB)


def shift(n, s):
    return [(i, (i + s) % n) for i in range(n)]


def swap_all(x, axis):
    return lax.all_to_all(x, axis, split_axis=0, concat_axis=0, tiled=True)


def split(x):
    hi = x.astype(bf16)
    return hi, (x - hi.astype(f32)).astype(bf16)


def dot(a, b):
    return jnp.dot(a, b, preferred_element_type=f32)


def dot3(a, b):
    ah, al = split(a)
    bh, bl = split(b)
    return dot(ah, bh) + (dot(ah, bl) + dot(al, bh))


def sort_kernel(owner, names, place, slot, inv):
    for node in range(2):

        def clear(t, _):
            inv[t] = -1
            return 0

        def mark(q, _):
            inv[owner[names[node, q]]] = q
            return 0

        def pick(g, _):
            t = 4 * g
            lo = jnp.where(inv[t] >= 0, 0, jnp.where(inv[t + 1] >= 0, 1, 2))
            hi = jnp.where(inv[t + 3] >= 0, 3, jnp.where(inv[t + 2] >= 0, 2, 1))
            place[node, 2 * g] = inv[t + lo]
            slot[node, 2 * g] = t + lo
            place[node, 2 * g + 1] = inv[t + hi]
            slot[node, 2 * g + 1] = t + hi
            return 0

        lax.fori_loop(0, 64, clear, 0)
        lax.fori_loop(0, 32, mark, 0)
        lax.fori_loop(0, 16, pick, 0)


def slice_kernel(up, low, out, buf, sems):
    copies = []
    for node in range(2):
        for q in range(4):
            for ul, src in enumerate((up, low)):
                copies.append(
                    pltpu.make_async_copy(
                        src.at[node, :, q * 32 : (q + 1) * 32, :], buf.at[node * 4 + q, ul], sems.at[len(copies)]
                    )
                )
    for c in copies:
        c.start()
    for c in copies:
        c.wait()
    whole = pltpu.make_async_copy(buf, out, sems.at[len(copies)])
    whole.start()
    whole.wait()


def order_kernel(pos, place, slot, ulen, llen, got, out, v0, v1, v2, v3, buf, sems):
    node, y = pos[0], pos[1]
    lens = (ulen[node], llen[node])
    lane = lax.broadcasted_iota(jnp.int32, (8, B), 1)
    info = jnp.zeros((8, B), f32)
    for s in range(32):
        info = jnp.where(lane == s, slot[node, s].astype(f32), info)
    copies = []
    for q in range(4):
        for h in range(2):
            for e in range(4):
                p = place[node, 16 * h + 4 * q + e]
                for ul in range(2):
                    at = pl.multiple_of((ul * 4 + (p & 3)) * 32, 32)
                    v = got[p >> 2, pl.ds(at, 32), :]
                    v = jnp.where(p < lens[ul], v, 0.0)
                    row = ((h * 4 + e) * 2 + ul) * 32
                    buf[q, row : row + 32, :] = v
        buf[q, 512:520, :] = info
        copies.append(pltpu.make_async_copy(buf.at[q], out.at[q], sems.at[q]))
        copies[-1].start()
    for i, v in enumerate((v0, v1, v2, v3)):
        copies.append(pltpu.make_async_copy(buf.at[(y + i) & 3, :512], v, sems.at[4 + i]))
        copies[-1].start()
    for c in copies:
        c.wait()


def fill(pos, lhi, llo, node, src, row, ys):
    xl, core = pos[2], pos[4]
    for p in range(4):
        half = xl if p < 2 else 1 - xl
        pair = core if p % 2 == 0 else 1 - core
        for b in range(2):
            e = half * 4 + pair * 2 + b
            for ul in range(2):
                r = pl.multiple_of((e * 2 + ul) * 32, 32)
                hi, lo = split(src[row, pl.ds(r, 32), :])
                at = pl.multiple_of((p * 2 + b) * B + ys * 32, 32)
                lhi[node, pl.ds(at, 32), ul * B : (ul + 1) * B] = hi
                llo[node, pl.ds(at, 32), ul * B : (ul + 1) * B] = lo


def fill_kernel(pos, l0, lu, ld, lhi, llo):
    y = pos[1]

    def step(node, _):
        fill(pos, lhi, llo, node, l0, node, y)
        fill(pos, lhi, llo, node, lu, node, (y + 3) & 3)
        fill(pos, lhi, llo, node, ld, node, (y + 1) & 3)
        return 0

    lax.fori_loop(0, 4, step, 0)


def product_kernel(first, *refs):
    if first:
        (pos, slots, lhi_in, llo_in, lf1, lf2, own, own_c, side, side_c,
         o0, o1, o2, o3, lhi, llo, *sel) = refs
        outs = ((2, o2), (1, o1), (3, o3), (0, o0))
        pieces = ((own,), (own_c,), (side,), (side_c,))
    else:
        (pos, slots, lhi, llo, top, bot, top_c, bot_c, side, side_c,
         o0, o1, o2, o3, *sel) = refs
        outs = ((2, o2), (1, o1), (3, o3), (0, o0))
        pieces = ((top, bot), (top_c, bot_c), (side,), (side_c,))
    h, y, xl, z, core = pos[0], pos[1], pos[2], pos[3], pos[4]
    at_half = (xl, xl, 1 - xl, 1 - xl)
    at_pair = (core, 1 - core, core, 1 - core)

    if first:

        def fill_far(i, _):
            fill(pos, lhi, llo, i, lf1, i, (y + 2) & 3)
            fill(pos, lhi, llo, i + 2, lf2, i, (y + 2) & 3)
            return 0

        lax.fori_loop(0, 2, fill_far, 0)

    m0 = 16 * (h if first else 1 - h) + 4 * y

    def select(k):
        node = (z + outs[k][0]) & 3
        selhi, sello = sel[2 * (k & 1)], sel[2 * (k & 1) + 1]
        for m in range(4):
            cm = slots[node, m0 + m] & 7
            for p in range(4):
                for b in range(2):
                    ck = slots[node, 16 * at_half[p] + 4 * z + 2 * at_pair[p] + b] & 3
                    lanes = pl.ds(pl.multiple_of(ck * B, B), B)
                    if len(pieces[p]) == 1:
                        blk = pieces[p][0][pl.ds(pl.multiple_of(cm * B, B), B), lanes]
                    else:
                        sub = pl.ds(pl.multiple_of((cm & 3) * B, B), B)
                        blk = jnp.where(cm < 4, pieces[p][0][sub, lanes], pieces[p][1][sub, lanes])
                    hi, lo = split(blk)
                    e = p * 2 + b
                    selhi[m * B : (m + 1) * B, e * B : (e + 1) * B] = hi
                    sello[m * B : (m + 1) * B, e * B : (e + 1) * B] = lo

    select(0)
    for k, (i, dst) in enumerate(outs):
        if k < 3:
            select(k + 1)
        node = (z + i) & 3
        ah, al = sel[2 * (k & 1)][...], sel[2 * (k & 1) + 1][...]
        bh, bl = lhi[node], llo[node]
        dst[...] = dot(ah, bh) + (dot(ah, bl) + dot(al, bh))


def product(first, *args):
    out = [shape(512, 256)] * 4
    if first:
        out = out + [jax.ShapeDtypeStruct((4, 1024, 256), bf16)] * 2
    return call(
        lambda *refs: product_kernel(first, *refs),
        out,
        [smem] * 2 + [vmem] * (len(args) - 2),
        [vmem] * len(out),
        [pltpu.VMEM((512, 1024), bf16)] * 4,
        mib=14,
        name="product_own" if first else "product_far",
        alias={2: 4, 3: 5} if first else {},
    )(*args)


def half_rows(h, y, rows, buf):
    for e in range(4):
        for i, src in enumerate(rows):
            to = pl.multiple_of(e * B + ((y - i) & 3) * 32, 32)
            for ul in range(2):
                at = pl.multiple_of(((h * 4 + e) * 2 + ul) * 32, 32)
                buf[pl.ds(to, 32), ul * B : (ul + 1) * B] = src[pl.ds(at, 32), :]
    return buf[...]


def far_kernel(o0, q1, q2, up, low):
    t = -(o0[...] + (q1[...] + q2[...])).T
    up[...] = t[:B]
    low[...] = t[B:]


def prods_kernel(pos, n0, q1, q2, up, low, v0, v1, v2, v3, near, prods, buf):
    h, y = pos[0], pos[1]
    rows = (v0, v1, v2, v3)
    t = -(n0[...] + (q1[...] + q2[...])).T
    near[...] = t
    s = dot3(t, half_rows(h, y, rows, buf))
    s = s + dot3(jnp.concatenate([up[...], low[...]], axis=0), half_rows(1 - h, y, rows, buf))
    prods[0] = s[:B, :B]
    prods[1] = s[:B, B:]
    prods[2] = s[B:, B:]


def rows_kernel(pos, place, slot, ulen, llen, mine, other_up, other_low, parent, up, low):
    h, y = pos[0], pos[1]
    r = h * 4 + y
    up[...] = jnp.zeros_like(up)
    low[...] = jnp.zeros_like(low)
    for k, src_up, src_low in ((0, mine.at[:B], mine.at[B:]), (1, other_up, other_low)):
        node = h if k == 0 else 1 - h
        lp = parent[node].T
        for e in range(4):
            p = place[node, 4 * r + e]
            at = pl.multiple_of((slot[node, 4 * r + e] & 7) * B, B)
            gu = jnp.where(p < ulen[node], src_up[:, e * B : (e + 1) * B], 0.0)
            gl = src_low[:, e * B : (e + 1) * B] - dot3(lp, gu)
            gl = jnp.where(p < llen[node], gl, 0.0)
            up[node, :, pl.ds(at, B)] = gu
            low[node, :, pl.ds(at, B)] = gl


def diag_kernel(pos, mine, other, uinv, linv, parent, du, pr, dl):
    h = pos[0]
    for k, src in ((0, mine), (1, other)):
        node = h if k == 0 else 1 - h
        lp = parent[node]
        lpt = lp.T
        cross = src[1]
        d = uinv[node] - src[0].T
        row = -(dot3(d, lp) + cross)
        low = src[2].T - dot3(cross.T, lp)
        du[node] = d
        pr[node] = row
        dl[node] = linv[node] - dot3(lpt, row) - low


def call(kernel, out_shape, in_specs, out_specs, scratch=(), mib=16, name=None, alias={}):
    return pl.pallas_call(
        kernel,
        out_shape=out_shape,
        in_specs=in_specs,
        out_specs=out_specs,
        scratch_shapes=list(scratch),
        compiler_params=params(mib),
        name=name,
        input_output_aliases=alias,
    )


def shape(*s):
    return jax.ShapeDtypeStruct(s, f32)


def body(
    ainv_top,
    block_owner,
    upper_list,
    upper_len,
    upper_panel,
    upper_dinv,
    lower_len,
    lower_panel,
    lower_parent,
    lower_dinv,
):
    pos = jnp.stack([lax.axis_index(n) for n in ("xh", "y", "xl", "z", "core")]).astype(jnp.int32)
    pp = lax.ppermute
    mirror = [(0, 3), (1, 2), (2, 1), (3, 0)]
    ints = jax.ShapeDtypeStruct((2, 32), jnp.int32)
    place, slot = call(
        sort_kernel, [ints] * 2, [smem] * 2, [smem] * 2, [pltpu.SMEM((64,), jnp.int32)], name="sort"
    )(block_owner, upper_list)
    sliced = call(
        slice_kernel, pltpu.HBM((8, 2, 4, 32, B), f32), [hbm] * 2, hbm, [pltpu.VMEM((8, 2, 4, 32, B), f32), pltpu.SemaphoreType.DMA((17,))], name="slices"
    )(
        pltpu.with_memory_space_constraint(upper_panel.reshape(2, 4, B, B), pltpu.HBM),
        pltpu.with_memory_space_constraint(lower_panel.reshape(2, 4, B, B), pltpu.HBM),
    )
    got = swap_all(sliced.reshape(8, 256, B), ROW)
    a = ainv_top
    a_nr = pp(a, "xl", shift(2, 1))
    a_fr = pp(a, RING, mirror)
    a_co = pp(a, "core", shift(2, 1))
    a_nr, a_fr = lax.optimization_barrier((a_nr, a_fr))
    got, a_co = lax.optimization_barrier((got, a_co))
    ordered, v0, v1, v2, v3 = call(
        order_kernel,
        [pltpu.HBM((4, 520, B), f32)] + [pltpu.HBM((512, B), f32)] * 4,
        [smem] * 5 + [vmem],
        [hbm] * 5,
        [pltpu.VMEM((4, 520, B), f32), pltpu.SemaphoreType.DMA((8,))],
        name="order",
    )(pos, place, slot, upper_len, lower_len, got)
    l0 = swap_all(ordered, "z")
    v1, v2, v3 = (pp(v, "y", shift(4, i + 1)) for i, v in enumerate((v1, v2, v3)))
    l0, v1, v3 = lax.optimization_barrier((l0, v1, v3))
    lu = pp(l0, "y", shift(4, 1))
    ld = pp(l0, "y", shift(4, 3))
    top, bottom, lu, ld = lax.optimization_barrier((a_nr[:512], a_fr[512:], lu, ld))
    a_f1 = pp(top, RING, mirror)
    a_f2 = pp(bottom, "xl", shift(2, 1))
    c_nr = pp(a_nr, "core", shift(2, 1))
    lf1 = pp(lu[:2], "y", shift(4, 1))
    lf2 = pp(ld[2:], "y", shift(4, 3))
    k_fr, lf1, lf2 = lax.optimization_barrier((a_fr, lf1, lf2))
    c_fr = pp(k_fr, "core", shift(2, 1))
    parts = jax.ShapeDtypeStruct((4, 1024, 256), bf16)
    hi, lo = call(fill_kernel, [parts] * 2, [smem] + [vmem] * 3, [vmem] * 2, mib=14, name="fill")(pos, l0, lu, ld)
    slots = l0[:, 512, :32].astype(jnp.int32)
    n0, n1, n2, n3, hi, lo = product(True, pos, slots, hi, lo, lf1, lf2, a, a_co, a_nr, c_nr)
    a_f1, a_f2, n0 = lax.optimization_barrier((a_f1, a_f2, n0))
    c_f1 = pp(a_f1, "core", shift(2, 1))
    c_f2 = pp(a_f2, "core", shift(2, 1))
    ra = pp(n2, "z", shift(4, 1))
    q3 = pp(n3, "z", shift(4, 3))
    o0, o1, o2, o3 = product(False, pos, slots, hi, lo, a_f1, a_f2, c_f1, c_f2, a_fr, c_fr)
    o1, ra = lax.optimization_barrier((o1, ra))
    o2, q3 = lax.optimization_barrier((o2, q3))
    q1 = pp(o1, "z", shift(4, 1))
    rb = pp(o2, "z", shift(4, 3))
    near_up = pp(n1 + ra, "z", shift(4, 1))
    far_dn = pp(o3 + rb, "z", shift(4, 3))
    far_up, far_low = call(far_kernel, [shape(B, 512)] * 2, [vmem] * 3, [vmem] * 2, mib=8, name="far")(o0, q1, far_dn)
    mine, prods = call(
        prods_kernel,
        [shape(256, 512), shape(3, B, B)],
        [smem] + [vmem] * 9,
        [vmem] * 2,
        [pltpu.VMEM((512, 256), f32)],
        mib=16,
        name="prods",
    )(pos, n0, near_up, q3, far_up, far_low, v0, v1, v2, v3)
    s1 = pp(prods, "y", shift(4, 1))
    s2 = pp(prods, "y", shift(4, 2))
    s3 = pp(prods, "y", shift(4, 3))
    other_up = pp(far_up, "xh", shift(2, 1))
    far_low, other_up = lax.optimization_barrier((far_low, other_up))
    other_low = pp(far_low, "xh", shift(2, 1))
    mine_sum = (prods + s1) + (s2 + s3)
    other_sum = pp(mine_sum, "xh", shift(2, 1))
    upper_rows, lower_rows = call(
        rows_kernel, [shape(2, B, 1024)] * 2, [smem] * 5 + [vmem] * 4, [vmem] * 2, name="rows"
    )(pos, place, slot, upper_len, lower_len, mine, other_up, other_low, lower_parent)
    other_sum, upper_rows = lax.optimization_barrier((other_sum, upper_rows))
    diag_up, parent_row, diag_low = call(
        diag_kernel, [shape(2, B, B)] * 3, [smem] + [vmem] * 5, [vmem] * 3, name="diag"
    )(pos, mine_sum, other_sum, upper_dinv, lower_dinv, lower_parent)
    return (upper_rows, diag_up, lower_rows, parent_row, diag_low)


def solution(mesh):
    fine = Mesh(mesh.devices.reshape(2, 4, 2, 4, 2), ("xh", "y", "xl", "z", "core"))
    row = ("xh", "y")
    col = ("xl", "z", "core")
    in_specs = (
        P(row, col),
        P(),
        P(col, None),
        P(col),
        P(col, row, None),
        P(col, None, None),
        P(col),
        P(col, row, None),
        P(col, None, None),
        P(col, None, None),
    )
    out_specs = (
        P(col, None, row),
        P(col, None, None),
        P(col, None, row),
        P(col, None, None),
        P(col, None, None),
    )
    return jax.shard_map(body, mesh=fine, in_specs=in_specs, out_specs=out_specs, check_vma=False)
```

```python
import jax
import jax.numpy as jnp
from jax import lax
from jax.experimental import pallas as pl
from jax.experimental.pallas import tpu as pltpu
from jax.sharding import Mesh, PartitionSpec as P

B = 128
MIB = 1 << 20
ROW = ("xh", "y")
RING = ("xh", "xl")
f32 = jnp.float32
bf16 = jnp.bfloat16

smem = pl.BlockSpec(memory_space=pltpu.SMEM)
vmem = pl.BlockSpec(memory_space=pltpu.VMEM)
hbm = pl.BlockSpec(memory_space=pltpu.HBM)


def params(mib):
    return pltpu.CompilerParams(vmem_limit_bytes=mib * MIB)


def shift(n, s):
    return [(i, (i + s) % n) for i in range(n)]


def swap_all(x, axis):
    return lax.all_to_all(x, axis, split_axis=0, concat_axis=0, tiled=True)


def split(x):
    hi = x.astype(bf16)
    return hi, (x - hi.astype(f32)).astype(bf16)


def dot(a, b):
    return jnp.dot(a, b, preferred_element_type=f32)


def dot3(a, b):
    ah, al = split(a)
    bh, bl = split(b)
    return dot(ah, bh) + (dot(ah, bl) + dot(al, bh))


def sort_kernel(owner, names, place, slot, inv):
    for node in range(2):

        def clear(t, _):
            inv[t] = -1
            return 0

        def mark(q, _):
            inv[owner[names[node, q]]] = q
            return 0

        def pick(g, _):
            t = 4 * g
            lo = jnp.where(inv[t] >= 0, 0, jnp.where(inv[t + 1] >= 0, 1, 2))
            hi = jnp.where(inv[t + 3] >= 0, 3, jnp.where(inv[t + 2] >= 0, 2, 1))
            place[node, 2 * g] = inv[t + lo]
            slot[node, 2 * g] = t + lo
            place[node, 2 * g + 1] = inv[t + hi]
            slot[node, 2 * g + 1] = t + hi
            return 0

        lax.fori_loop(0, 64, clear, 0)
        lax.fori_loop(0, 32, mark, 0)
        lax.fori_loop(0, 16, pick, 0)


def slice_kernel(up, low, out, buf, sems):
    copies = []
    for node in range(2):
        for q in range(4):
            for ul, src in enumerate((up, low)):
                copies.append(
                    pltpu.make_async_copy(
                        src.at[node, :, q * 32 : (q + 1) * 32, :], buf.at[node * 4 + q, ul], sems.at[len(copies)]
                    )
                )
    for c in copies:
        c.start()
    for c in copies:
        c.wait()
    whole = pltpu.make_async_copy(buf, out, sems.at[len(copies)])
    whole.start()
    whole.wait()


def order_kernel(pos, place, slot, ulen, llen, got, out, v0, v1, v2, v3, buf, sems):
    node, y = pos[0], pos[1]
    lens = (ulen[node], llen[node])
    lane = lax.broadcasted_iota(jnp.int32, (8, B), 1)
    info = jnp.zeros((8, B), f32)
    for s in range(32):
        info = jnp.where(lane == s, slot[node, s].astype(f32), info)
    copies = []
    for q in range(4):
        for h in range(2):
            for e in range(4):
                p = place[node, 16 * h + 4 * q + e]
                for ul in range(2):
                    at = pl.multiple_of((ul * 4 + (p & 3)) * 32, 32)
                    v = got[p >> 2, pl.ds(at, 32), :]
                    v = jnp.where(p < lens[ul], v, 0.0)
                    row = ((h * 4 + e) * 2 + ul) * 32
                    buf[q, row : row + 32, :] = v
        buf[q, 512:520, :] = info
        copies.append(pltpu.make_async_copy(buf.at[q], out.at[q], sems.at[q]))
        copies[-1].start()
    for i, v in enumerate((v0, v1, v2, v3)):
        copies.append(pltpu.make_async_copy(buf.at[(y + i) & 3, :512], v, sems.at[4 + i]))
        copies[-1].start()
    for c in copies:
        c.wait()


def fill(pos, lhi, llo, node, src, row, ys):
    xl, core = pos[2], pos[4]
    for p in range(4):
        half = xl if p < 2 else 1 - xl
        pair = core if p % 2 == 0 else 1 - core
        for b in range(2):
            e = half * 4 + pair * 2 + b
            for ul in range(2):
                r = pl.multiple_of((e * 2 + ul) * 32, 32)
                hi, lo = split(src[row, pl.ds(r, 32), :])
                at = pl.multiple_of((p * 2 + b) * B + ys * 32, 32)
                lhi[node, pl.ds(at, 32), ul * B : (ul + 1) * B] = hi
                llo[node, pl.ds(at, 32), ul * B : (ul + 1) * B] = lo


def fill_kernel(pos, l0, lu, ld, lhi, llo):
    y = pos[1]

    def step(node, _):
        fill(pos, lhi, llo, node, l0, node, y)
        fill(pos, lhi, llo, node, lu, node, (y + 3) & 3)
        fill(pos, lhi, llo, node, ld, node, (y + 1) & 3)
        return 0

    lax.fori_loop(0, 4, step, 0)


def product_kernel(first, *refs):
    if first:
        (pos, slots, lhi_in, llo_in, lf1, lf2, own, own_c, side, side_c,
         o0, o1, o2, o3, lhi, llo, *sel) = refs
        outs = ((2, o2), (1, o1), (3, o3), (0, o0))
        pieces = ((own,), (own_c,), (side,), (side_c,))
    else:
        (pos, slots, lhi, llo, top, bot, top_c, bot_c, side, side_c,
         o0, o1, o2, o3, *sel) = refs
        outs = ((2, o2), (1, o1), (3, o3), (0, o0))
        pieces = ((top, bot), (top_c, bot_c), (side,), (side_c,))
    h, y, xl, z, core = pos[0], pos[1], pos[2], pos[3], pos[4]
    at_half = (xl, xl, 1 - xl, 1 - xl)
    at_pair = (core, 1 - core, core, 1 - core)

    if first:

        def fill_far(i, _):
            fill(pos, lhi, llo, i, lf1, i, (y + 2) & 3)
            fill(pos, lhi, llo, i + 2, lf2, i, (y + 2) & 3)
            return 0

        lax.fori_loop(0, 2, fill_far, 0)

    m0 = 16 * (h if first else 1 - h) + 4 * y

    def select(k):
        node = (z + outs[k][0]) & 3
        selhi, sello = sel[2 * (k & 1)], sel[2 * (k & 1) + 1]
        for m in range(4):
            cm = slots[node, m0 + m] & 7
            for p in range(4):
                for b in range(2):
                    ck = slots[node, 16 * at_half[p] + 4 * z + 2 * at_pair[p] + b] & 3
                    lanes = pl.ds(pl.multiple_of(ck * B, B), B)
                    if len(pieces[p]) == 1:
                        blk = pieces[p][0][pl.ds(pl.multiple_of(cm * B, B), B), lanes]
                    else:
                        sub = pl.ds(pl.multiple_of((cm & 3) * B, B), B)
                        blk = jnp.where(cm < 4, pieces[p][0][sub, lanes], pieces[p][1][sub, lanes])
                    hi, lo = split(blk)
                    e = p * 2 + b
                    selhi[m * B : (m + 1) * B, e * B : (e + 1) * B] = hi
                    sello[m * B : (m + 1) * B, e * B : (e + 1) * B] = lo

    select(0)
    for k, (i, dst) in enumerate(outs):
        if k < 3:
            select(k + 1)
        node = (z + i) & 3
        ah, al = sel[2 * (k & 1)][...], sel[2 * (k & 1) + 1][...]
        bh, bl = lhi[node], llo[node]
        dst[...] = dot(ah, bh) + (dot(ah, bl) + dot(al, bh))


def product(first, *args):
    out = [shape(512, 256)] * 4
    if first:
        out = out + [jax.ShapeDtypeStruct((4, 1024, 256), bf16)] * 2
    return call(
        lambda *refs: product_kernel(first, *refs),
        out,
        [smem] * 2 + [vmem] * (len(args) - 2),
        [vmem] * len(out),
        [pltpu.VMEM((512, 1024), bf16)] * 4,
        mib=14,
        name="product_own" if first else "product_far",
        alias={2: 4, 3: 5} if first else {},
    )(*args)


def half_rows(h, y, rows, buf):
    for e in range(4):
        for i, src in enumerate(rows):
            to = pl.multiple_of(e * B + ((y - i) & 3) * 32, 32)
            for ul in range(2):
                at = pl.multiple_of(((h * 4 + e) * 2 + ul) * 32, 32)
                buf[pl.ds(to, 32), ul * B : (ul + 1) * B] = src[pl.ds(at, 32), :]
    return buf[...]


def far_kernel(o0, q1, q2, up, low):
    t = -(o0[...] + (q1[...] + q2[...])).T
    up[...] = t[:B]
    low[...] = t[B:]


def prods_kernel(pos, n0, q1, q2, up, low, v0, v1, v2, v3, near, prods, buf):
    h, y = pos[0], pos[1]
    rows = (v0, v1, v2, v3)
    t = -(n0[...] + (q1[...] + q2[...])).T
    near[...] = t
    s = dot3(t, half_rows(h, y, rows, buf))
    s = s + dot3(jnp.concatenate([up[...], low[...]], axis=0), half_rows(1 - h, y, rows, buf))
    prods[0] = s[:B, :B]
    prods[1] = s[:B, B:]
    prods[2] = s[B:, B:]


def rows_kernel(pos, place, slot, ulen, llen, mine, other_up, other_low, parent, up, low):
    h, y = pos[0], pos[1]
    r = h * 4 + y
    up[...] = jnp.zeros_like(up)
    low[...] = jnp.zeros_like(low)
    for k, src_up, src_low in ((0, mine.at[:B], mine.at[B:]), (1, other_up, other_low)):
        node = h if k == 0 else 1 - h
        lp = parent[node].T
        for e in range(4):
            p = place[node, 4 * r + e]
            at = pl.multiple_of((slot[node, 4 * r + e] & 7) * B, B)
            gu = jnp.where(p < ulen[node], src_up[:, e * B : (e + 1) * B], 0.0)
            gl = src_low[:, e * B : (e + 1) * B] - dot3(lp, gu)
            gl = jnp.where(p < llen[node], gl, 0.0)
            up[node, :, pl.ds(at, B)] = gu
            low[node, :, pl.ds(at, B)] = gl


def diag_kernel(pos, mine, other, uinv, linv, parent, du, pr, dl):
    h = pos[0]
    for k, src in ((0, mine), (1, other)):
        node = h if k == 0 else 1 - h
        lp = parent[node]
        lpt = lp.T
        cross = src[1]
        d = uinv[node] - src[0].T
        row = -(dot3(d, lp) + cross)
        low = src[2].T - dot3(cross.T, lp)
        du[node] = d
        pr[node] = row
        dl[node] = linv[node] - dot3(lpt, row) - low


def call(kernel, out_shape, in_specs, out_specs, scratch=(), mib=16, name=None, alias={}):
    return pl.pallas_call(
        kernel,
        out_shape=out_shape,
        in_specs=in_specs,
        out_specs=out_specs,
        scratch_shapes=list(scratch),
        compiler_params=params(mib),
        name=name,
        input_output_aliases=alias,
    )


def shape(*s):
    return jax.ShapeDtypeStruct(s, f32)


def body(
    ainv_top,
    block_owner,
    upper_list,
    upper_len,
    upper_panel,
    upper_dinv,
    lower_len,
    lower_panel,
    lower_parent,
    lower_dinv,
):
    pos = jnp.stack([lax.axis_index(n) for n in ("xh", "y", "xl", "z", "core")]).astype(jnp.int32)
    pp = lax.ppermute
    mirror = [(0, 3), (1, 2), (2, 1), (3, 0)]
    ints = jax.ShapeDtypeStruct((2, 32), jnp.int32)
    place, slot = call(
        sort_kernel, [ints] * 2, [smem] * 2, [smem] * 2, [pltpu.SMEM((64,), jnp.int32)], name="sort"
    )(block_owner, upper_list)
    sliced = call(
        slice_kernel, pltpu.HBM((8, 2, 4, 32, B), f32), [hbm] * 2, hbm, [pltpu.VMEM((8, 2, 4, 32, B), f32), pltpu.SemaphoreType.DMA((17,))], name="slices"
    )(
        pltpu.with_memory_space_constraint(upper_panel.reshape(2, 4, B, B), pltpu.HBM),
        pltpu.with_memory_space_constraint(lower_panel.reshape(2, 4, B, B), pltpu.HBM),
    )
    got = swap_all(sliced.reshape(8, 256, B), ROW)
    a = ainv_top
    a_nr = pp(a, "xl", shift(2, 1))
    a_fr = pp(a, RING, mirror)
    a_co = pp(a, "core", shift(2, 1))
    a_nr, a_fr = lax.optimization_barrier((a_nr, a_fr))
    got, a_co = lax.optimization_barrier((got, a_co))
    ordered, v0, v1, v2, v3 = call(
        order_kernel,
        [pltpu.HBM((4, 520, B), f32)] + [pltpu.HBM((512, B), f32)] * 4,
        [smem] * 5 + [vmem],
        [hbm] * 5,
        [pltpu.VMEM((4, 520, B), f32), pltpu.SemaphoreType.DMA((8,))],
        name="order",
    )(pos, place, slot, upper_len, lower_len, got)
    l0 = swap_all(ordered, "z")
    v1, v2, v3 = (pp(v, "y", shift(4, i + 1)) for i, v in enumerate((v1, v2, v3)))
    lu = pp(l0, "y", shift(4, 1))
    ld = pp(l0, "y", shift(4, 3))
    top, bottom, lu, ld = lax.optimization_barrier((a_nr[:512], a_fr[512:], lu, ld))
    a_f1 = pp(top, RING, mirror)
    a_f2 = pp(bottom, "xl", shift(2, 1))
    c_nr = pp(a_nr, "core", shift(2, 1))
    lf1 = pp(lu[:2], "y", shift(4, 1))
    lf2 = pp(ld[2:], "y", shift(4, 3))
    k_fr, lf1, lf2 = lax.optimization_barrier((a_fr, lf1, lf2))
    c_fr = pp(k_fr, "core", shift(2, 1))
    parts = jax.ShapeDtypeStruct((4, 1024, 256), bf16)
    hi, lo = call(fill_kernel, [parts] * 2, [smem] + [vmem] * 3, [vmem] * 2, mib=14, name="fill")(pos, l0, lu, ld)
    slots = l0[:, 512, :32].astype(jnp.int32)
    n0, n1, n2, n3, hi, lo = product(True, pos, slots, hi, lo, lf1, lf2, a, a_co, a_nr, c_nr)
    a_f1, a_f2, n0 = lax.optimization_barrier((a_f1, a_f2, n0))
    c_f1 = pp(a_f1, "core", shift(2, 1))
    c_f2 = pp(a_f2, "core", shift(2, 1))
    ra = pp(n2, "z", shift(4, 1))
    q3 = pp(n3, "z", shift(4, 3))
    o0, o1, o2, o3 = product(False, pos, slots, hi, lo, a_f1, a_f2, c_f1, c_f2, a_fr, c_fr)
    o1, ra = lax.optimization_barrier((o1, ra))
    o2, q3 = lax.optimization_barrier((o2, q3))
    q1 = pp(o1, "z", shift(4, 1))
    rb = pp(o2, "z", shift(4, 3))
    near_up = pp(n1 + ra, "z", shift(4, 1))
    far_dn = pp(o3 + rb, "z", shift(4, 3))
    far_up, far_low = call(far_kernel, [shape(B, 512)] * 2, [vmem] * 3, [vmem] * 2, mib=8, name="far")(o0, q1, far_dn)
    mine, prods = call(
        prods_kernel,
        [shape(256, 512), shape(3, B, B)],
        [smem] + [vmem] * 9,
        [vmem] * 2,
        [pltpu.VMEM((512, 256), f32)],
        mib=16,
        name="prods",
    )(pos, n0, near_up, q3, far_up, far_low, v0, v1, v2, v3)
    s1 = pp(prods, "y", shift(4, 1))
    s2 = pp(prods, "y", shift(4, 2))
    s3 = pp(prods, "y", shift(4, 3))
    other_up = pp(far_up, "xh", shift(2, 1))
    far_low, other_up = lax.optimization_barrier((far_low, other_up))
    other_low = pp(far_low, "xh", shift(2, 1))
    mine_sum = (prods + s1) + (s2 + s3)
    other_sum = pp(mine_sum, "xh", shift(2, 1))
    upper_rows, lower_rows = call(
        rows_kernel, [shape(2, B, 1024)] * 2, [smem] * 5 + [vmem] * 4, [vmem] * 2, name="rows"
    )(pos, place, slot, upper_len, lower_len, mine, other_up, other_low, lower_parent)
    other_sum, upper_rows = lax.optimization_barrier((other_sum, upper_rows))
    diag_up, parent_row, diag_low = call(
        diag_kernel, [shape(2, B, B)] * 3, [smem] + [vmem] * 5, [vmem] * 3, name="diag"
    )(pos, mine_sum, other_sum, upper_dinv, lower_dinv, lower_parent)
    return (upper_rows, diag_up, lower_rows, parent_row, diag_low)


def solution(mesh):
    fine = Mesh(mesh.devices.reshape(2, 4, 2, 4, 2), ("xh", "y", "xl", "z", "core"))
    row = ("xh", "y")
    col = ("xl", "z", "core")
    in_specs = (
        P(row, col),
        P(),
        P(col, None),
        P(col),
        P(col, row, None),
        P(col, None, None),
        P(col),
        P(col, row, None),
        P(col, None, None),
        P(col, None, None),
    )
    out_specs = (
        P(col, None, row),
        P(col, None, None),
        P(col, None, row),
        P(col, None, None),
        P(col, None, None),
    )
    return jax.shard_map(body, mesh=fine, in_specs=in_specs, out_specs=out_specs, check_vma=False)
```
